32 devices in a mesh: dp: 2 (over x), tm: 4 (over y, core), height: 4 (over z).
Axes of the slice: x: 2, y: 2, z: 4, core: 2. Of those that a mesh axis runs over, the one named last changes fastest.
Arguments:
- frames_in: bfloat16 [2, 12, 12, 320, 128], P('dp', 'tm', 'height'), may hold values from -6 to 6
- grad_out: bfloat16 [2, 12, 12, 320, 128], P('dp', 'tm', 'height'), may hold values from -6 to 6
- w_spatial: bfloat16 [3, 3, 128, 128], replicated, may hold values from -0.1875 to 0.1875
- w_temporal: bfloat16 [3, 128, 128], replicated, may hold values from -0.3125 to 0.3125
Outputs:
- layer_out: bfloat16 [2, 12, 12, 320, 128], P('dp', 'tm', 'height')
- grad_in: bfloat16 [2, 12, 12, 320, 128], P('dp', 'tm', 'height')
- grad_spatial: float32 [3, 3, 128, 128], replicated
- grad_temporal: float32 [3, 128, 128], replicated
The draws below stay inside these ranges and needn't reach their ends.
All inputs are finite; a program needn't handle non-finite values.
Results may differ from the reference program's by a relative error of at most 0.005.
Values may be sent and summed in bfloat16 or wider, within the bound.
A program may use at most 64 MiB of HBM per device.

```python
import math
import jax
import jax.numpy as jnp
from jax import lax

C = 128
COLS = 320
CLIPS = 2
FRAMES = 12
ROWS = 12
PIXELS = 92160


def levels(stream_key, shape, shards, low, high):
    def one(dim, blocks):
        steps = jax.random.uniform(jax.random.fold_in(jax.random.fold_in(stream_key, 6), dim), (blocks,), jnp.float32, low / len(shards), high / len(shards))
        return jnp.repeat(jnp.exp(steps), shape[dim] // blocks).reshape((-1,) + (1,) * (len(shape) - dim - 1))

    loudness = one(*shards[0])
    for cut in shards[1:]:
        loudness = loudness * one(*cut)
    return loudness


def centred(rng, shape, width, reach, shards=(), held_as=jnp.bfloat16):
    array = jax.random.normal(rng, shape, jnp.float32) * width
    if len(shards) > 0:
        array = levels(rng, shape, shards, -0.22, 0.18) * array
    return jnp.clip(array, min=-reach, max=reach).astype(held_as)


def setup_inputs(seed: int = 0) -> dict:
    streams_of = jax.random.split(jax.random.key(seed), 5)
    frames_in = centred(streams_of[0], (CLIPS, FRAMES, ROWS, COLS, C), 1.0, 6.0, ((0, 2), (1, 4), (2, 4)))
    grad_out = centred(streams_of[1], (CLIPS, FRAMES, ROWS, COLS, C), 1.0, 6.0, ((0, 2), (1, 4), (2, 4)))
    w_spatial = centred(streams_of[2], (3, 3, C, C), (9 * C) ** -0.5, 0.1875)
    w_temporal = centred(streams_of[3], (3, C, C), (3 * C) ** -0.5, 0.3125)
    return {"frames_in": frames_in, "grad_out": grad_out, "w_spatial": w_spatial, "w_temporal": w_temporal}


def reference(frames_in, grad_out, w_spatial, w_temporal):
    spatial_f = w_spatial.astype(jnp.float32)
    temporal_f = w_temporal.astype(jnp.float32)

    def clip_step(carry, pair):
        clip_x, clip_g = pair
        padded_x = jnp.pad(clip_x, ((0, 0), (1, 1), (1, 1), (0, 0))).astype(jnp.float32)
        pre_act = jnp.zeros((FRAMES, ROWS, COLS, C), jnp.float32)
        for row_tap in range(3):
            for col_tap in range(3):
                pre_act = pre_act + jnp.einsum('frwc,cd->frwd', padded_x[:, row_tap:row_tap + ROWS, col_tap:col_tap + COLS], spatial_f[row_tap, col_tap])
        hidden = jax.nn.silu(pre_act).astype(jnp.bfloat16)
        hidden_pad = jnp.pad(hidden, ((2, 0), (0, 0), (0, 0), (0, 0))).astype(jnp.float32)
        mixed = jnp.zeros((FRAMES, ROWS, COLS, C), jnp.float32)
        for lag_tap in range(3):
            mixed = mixed + jnp.einsum('frwc,cd->frwd', hidden_pad[2 - lag_tap:2 - lag_tap + FRAMES], temporal_f[lag_tap])
        grad_full = clip_g.astype(jnp.float32)
        grad_pad = jnp.pad(grad_full, ((0, 2), (0, 0), (0, 0), (0, 0)))
        grad_hidden = jnp.zeros((FRAMES, ROWS, COLS, C), jnp.float32)
        for lag_tap in range(3):
            grad_hidden = grad_hidden + jnp.einsum('frwd,cd->frwc', grad_pad[lag_tap:lag_tap + FRAMES], temporal_f[lag_tap])
        temporal_part = jnp.stack([jnp.einsum('frwc,frwd->cd', hidden_pad[2 - lag_tap:2 - lag_tap + FRAMES], grad_full) for lag_tap in range(3)])
        sigma = jax.nn.sigmoid(pre_act)
        grad_pre = (grad_hidden * sigma * (1.0 + pre_act * (1.0 - sigma))).astype(jnp.bfloat16)
        grad_pre_f = grad_pre.astype(jnp.float32)
        grad_pre_pad = jnp.pad(grad_pre_f, ((0, 0), (1, 1), (1, 1), (0, 0)))
        grad_input = jnp.zeros((FRAMES, ROWS, COLS, C), jnp.float32)
        for row_tap in range(3):
            for col_tap in range(3):
                grad_input = grad_input + jnp.einsum('frwd,cd->frwc', grad_pre_pad[:, 2 - row_tap:2 - row_tap + ROWS, 2 - col_tap:2 - col_tap + COLS], spatial_f[row_tap, col_tap])
        spatial_part = jnp.stack([jnp.stack([jnp.einsum('frwc,frwd->cd', padded_x[:, row_tap:row_tap + ROWS, col_tap:col_tap + COLS], grad_pre_f) for col_tap in range(3)]) for row_tap in range(3)])
        new_carry = (carry[0] + spatial_part, carry[1] + temporal_part)
        return (new_carry, (mixed.astype(jnp.bfloat16), grad_input.astype(jnp.bfloat16)))
    start = (jnp.zeros((3, 3, C, C), jnp.float32), jnp.zeros((3, C, C), jnp.float32))
    sums, outputs = lax.scan(clip_step, start, (frames_in, grad_out))
    factor = 1.0 / math.sqrt(PIXELS)
    return (outputs[0], outputs[1], sums[0] * factor, sums[1] * factor)
```

```python
import functools
import math

import jax
import jax.numpy as jnp
from jax import lax
from jax.experimental import pallas as pl
from jax.experimental.pallas import tpu as pltpu
from jax.sharding import PartitionSpec as P

F32, BF16 = jnp.float32, jnp.bfloat16
MESH = pl.DeviceIdType.MESH
SPATIAL_CHUNKS = 3


def tdot(lhs, rhs):
    return lax.dot_general(lhs, rhs, (((0,), (0,)), ((), ())), preferred_element_type=F32)


def dot(lhs, rhs):
    return jnp.dot(lhs, rhs, preferred_element_type=F32)


class Plan:
    def __init__(self, sizes, ch):
        self.n_dp, self.n_tm, self.n_h = sizes
        self.fold = self.n_dp == 2
        self.n1 = self.n_tm * (self.n_dp if self.fold else 1)
        self.n2 = self.n_h * (1 if self.fold else self.n_dp)
        size = 9 * ch // SPATIAL_CHUNKS
        self.chunks = [(size * k, size) for k in range(SPATIAL_CHUNKS)] + [(9 * ch, 3 * ch)]
        self.piece = max(rows for _, rows in self.chunks) // self.n1
        self.offsets1 = [
            (a, b, c) for a in ((1, 0) if self.fold else (0,)) for b in (1, 0) for c in (0, 1) if a + b + c
        ]


def kernel(
    plan, dims, factor,
    x_hbm, g_hbm, ws_hbm, wt_hbm,
    lo_hbm, gi_hbm, res_hbm,
    ws_ref, wt_ref, x_ext, xs, g_ext, hid, gp, gps, wf, wb, wtb, pre_s, gh_s, acc, part, slot1, slot2, fin, lo, gi,
    loc, xh_s, xh_r, gh_sem, gh_r, hd_s, hd_r, gp_s, gp_r, s1_s, s1_r, s2_s, s2_r, s3_s, s3_r,
):
    n_dp, n_tm, n_h = plan.n_dp, plan.n_tm, plan.n_h
    frames, rows, cols, ch = dims
    pix = rows * cols
    me_dp, me_tm, me_h = lax.axis_index("dp"), lax.axis_index("tm"), lax.axis_index("height")

    def remote(src, dst, send, recv, device):
        return pltpu.make_async_remote_copy(
            src_ref=src, dst_ref=dst, send_sem=send, recv_sem=recv, device_id=device, device_id_type=MESH,
        )

    x_in = pltpu.make_async_copy(x_hbm.at[0], x_ext.at[:, pl.ds(1, rows)], loc.at[0])
    g_in = pltpu.make_async_copy(g_hbm.at[0], g_ext.at[pl.ds(0, frames)], loc.at[1])
    ws_in = pltpu.make_async_copy(ws_hbm, ws_ref, loc.at[2])
    wt_in = pltpu.make_async_copy(wt_hbm, wt_ref, loc.at[3])
    x_in.start()
    ws_in.start()
    wt_in.start()
    g_in.start()

    me_y, me_core = lax.div(me_tm, 2), lax.rem(me_tm, 2)

    def peer1(offset):
        a, b, c = offset
        dp = lax.rem(me_dp + a, 2) if plan.fold else me_dp
        tm = 2 * lax.rem(me_y + b, 2) + lax.rem(me_core + c, 2)
        return {"dp": dp, "tm": tm}, (dp * n_tm + tm if plan.fold else tm)

    me1 = me_dp * n_tm + me_tm if plan.fold else me_tm
    me2 = me_h if plan.fold else me_dp * n_h + me_h

    def peer2(step):
        index = lax.rem(me2 + step, plan.n2)
        if plan.fold:
            return {"height": index}, index
        return {"dp": lax.div(index, n_h), "height": lax.rem(index, n_h)}, index

    barrier = pltpu.get_barrier_semaphore()
    for step in range(1, plan.n2):
        pl.semaphore_signal(barrier, inc=1, device_id=peer2(step)[0], device_id_type=MESH)
    for offset in plan.offsets1:
        pl.semaphore_signal(barrier, inc=1, device_id=peer1(offset)[0], device_id_type=MESH)

    has_up, has_down = me_h > 0, me_h < n_h - 1
    has_prev, has_next = me_tm > 0, me_tm < n_tm - 1
    up, down = lax.rem(me_h + n_h - 1, n_h), lax.rem(me_h + 1, n_h)
    prev, nxt = lax.rem(me_tm + n_tm - 1, n_tm), lax.rem(me_tm + 1, n_tm)

    def x_copy(f, side):
        if side == 0:
            return remote(
                x_hbm.at[0, f, rows - 1], x_ext.at[f, 0], xh_s.at[f, 0], xh_r.at[f, 0], {"height": down}
            )
        return remote(x_hbm.at[0, f, 0], x_ext.at[f, rows + 1], xh_s.at[f, 1], xh_r.at[f, 1], {"height": up})

    def g_copy(f):
        return remote(g_hbm.at[0, f], g_ext.at[frames + f], gh_sem.at[f], gh_r.at[f], {"tm": prev})

    def h_copy(f):
        return remote(hid.at[f + 2], hid.at[f + 2 - frames], hd_s.at[f], hd_r.at[f], {"tm": nxt})

    def p_copy(f, side):
        if side == 0:
            return remote(gp.at[f, rows], gp.at[f, 0], gp_s.at[f, 0], gp_r.at[f, 0], {"height": down})
        return remote(gp.at[f, 1], gp.at[f, rows + 1], gp_s.at[f, 1], gp_r.at[f, 1], {"height": up})

    @pl.when(me_h == 0)
    def _():
        x_ext[:, 0] = jnp.zeros((frames, cols, ch), BF16)
        gp[:, 0] = jnp.zeros((frames, cols, ch), BF16)

    @pl.when(me_h == n_h - 1)
    def _():
        x_ext[:, rows + 1] = jnp.zeros((frames, cols, ch), BF16)
        gp[:, rows + 1] = jnp.zeros((frames, cols, ch), BF16)

    @pl.when(me_tm == 0)
    def _():
        hid[pl.ds(0, 2)] = jnp.zeros((2, rows, cols, ch), BF16)

    @pl.when(me_tm == n_tm - 1)
    def _():
        g_ext[pl.ds(frames, 2)] = jnp.zeros((2, rows, cols, ch), BF16)

    place = lax.broadcasted_iota(jnp.int32, (cols, ch), 0)

    def stack(source, target, f, r):
        value = source[f, r]
        wide = value.astype(F32)
        left = jnp.where(place == 0, 0.0, pltpu.roll(wide, 1, 0))
        right = jnp.where(place == cols - 1, 0.0, pltpu.roll(wide, cols - 1, 0))
        target[f, r, :, pl.ds(0, ch)] = left.astype(BF16)
        target[f, r, :, pl.ds(ch, ch)] = value
        target[f, r, :, pl.ds(2 * ch, ch)] = right.astype(BF16)

    def spread(source, weights, f, sources):
        sums = {}
        for s in sources:
            first, last = max(1, s - 1), min(rows, s + 1)
            at = first - s + 1
            wide = dot(source[f, s], weights[:, at * ch : (at + last - first + 1) * ch])
            for r in range(first, last + 1):
                term = wide[:, (r - first) * ch : (r - first + 1) * ch]
                sums[r] = sums[r] + term if r in sums else term
        return sums

    def beside(parts):
        return jnp.concatenate([p.reshape(pix, ch) for p in parts], axis=1)

    x_in.wait()

    @pl.loop(0, frames)
    def _(f):
        for r in range(1, rows + 1):
            stack(x_ext, xs, f, r)

    pl.semaphore_wait(barrier, plan.n2 - 1 + len(plan.offsets1))
    for f in range(frames):
        pl.when(has_down)(x_copy(f, 0).start)
        pl.when(has_up)(x_copy(f, 1).start)
    for f in range(2):
        pl.when(has_prev)(g_copy(f).start)

    ws_in.wait()
    wt_in.wait()
    for i in range(3):
        wf[:, pl.ds((2 - i) * ch, ch)] = ws_ref[i].reshape(3 * ch, ch)
        for j in range(3):
            wb[pl.ds((2 - j) * ch, ch), pl.ds(i * ch, ch)] = ws_ref[i, j].T
        wtb[pl.ds(i * ch, ch)] = wt_ref[i].T

    @pl.loop(0, frames)
    def _(f):
        for r, value in spread(xs, wf, f, range(1, rows + 1)).items():
            pre_s[f, r - 1] = value

    g_in.wait()
    for f in range(frames):
        near = min(3, frames - f)
        value = dot(beside([g_ext[f + k] for k in range(near)]), wtb[pl.ds(0, near * ch)])
        gh_s[f] = value.reshape(rows, cols, ch)

    acc[...] = jnp.zeros(acc.shape, F32)

    def frame(f):
        pl.when(has_up)(x_copy(f, 0).wait_recv)
        pl.when(has_down)(x_copy(f, 1).wait_recv)
        near = min(3, frames - f)
        if near < 3:
            pl.when(has_next)(g_copy(2 - near).wait_recv)
        for r in (0, rows + 1):
            stack(x_ext, xs, f, r)
        edge = spread(xs, wf, f, (0, rows + 1))
        far = None
        if near < 3:
            far = dot(beside([g_ext[f + k] for k in range(near, 3)]), wtb[pl.ds(near * ch, (3 - near) * ch)])
            far = far.reshape(rows, cols, ch)
        for r in range(1, rows + 1):
            pre = pre_s[f, r - 1]
            if r in edge:
                pre = pre + edge[r]
            sigma = jax.nn.sigmoid(pre)
            hid[f + 2, r - 1] = (pre * sigma).astype(BF16)
            grad_hidden = gh_s[f, r - 1]
            if far is not None:
                grad_hidden = grad_hidden + far[r - 1]
            grad_pre = grad_hidden * sigma * (1.0 + pre * (1.0 - sigma))
            gp[f, r] = grad_pre.astype(BF16)
            stack(gp, gps, f, r)
        pl.when(has_down)(p_copy(f, 0).start)
        pl.when(has_up)(p_copy(f, 1).start)

    def temporal_grad(f):
        term = tdot(hid[f + 2].reshape(pix, ch), beside([g_ext[f + k] for k in range(3)]))
        for k in range(3):
            acc[pl.ds((9 + k) * ch, ch)] += term[:, k * ch : (k + 1) * ch]

    def spatial_grad(f):
        term = tdot(
            beside([x_ext[f, pl.ds(i, rows)] for i in range(3)]),
            gps[f, pl.ds(1, rows)].reshape(pix, 3 * ch),
        )
        for j in range(3):
            acc[pl.ds(3 * j * ch, 3 * ch)] += term[:, (2 - j) * ch : (3 - j) * ch]

    n_chunks = len(plan.chunks)
    temporal = n_chunks - 1

    def s1_copy(c, k):
        base, size = plan.chunks[c]
        piece = size // plan.n1
        device, index = peer1(plan.offsets1[k])
        return remote(
            part.at[pl.ds(pl.multiple_of(base + index * piece, 16), piece)],
            slot1.at[c, k, pl.ds(0, piece)], s1_s.at[c, k], s1_r.at[c, k], device,
        )

    def scatter(c):
        base, size = plan.chunks[c]
        part[pl.ds(base, size)] = acc[pl.ds(base, size)].astype(BF16)
        for k in range(len(plan.offsets1)):
            s1_copy(c, k).start()

    def s2_copy(c, step):
        piece = plan.chunks[c][1] // plan.n1
        device, _ = peer2(step)
        at = slot2.at[c, me2, pl.ds(0, piece)]
        return remote(at, at, s2_s.at[c, step - 1], s2_r.at[c, me2], device)

    def s2_from(c, step):
        piece = plan.chunks[c][1] // plan.n1
        device, index = peer2(step)
        at = slot2.at[c, index, pl.ds(0, piece)]
        return remote(at, at, s2_s.at[c, step - 1], s2_r.at[c, index], device)

    def exchange(c):
        base, size = plan.chunks[c]
        piece = size // plan.n1
        total = acc[pl.ds(pl.multiple_of(base + me1 * piece, 16), piece)]
        for k in range(len(plan.offsets1)):
            s1_copy(c, k).wait_recv()
            total = total + slot1[c, k, pl.ds(0, piece)].astype(F32)
        slot2[c, me2, pl.ds(0, piece)] = total.astype(BF16)
        for step in range(1, plan.n2):
            s2_copy(c, step).start()

    def s3_copy(c, k):
        base, size = plan.chunks[c]
        piece = size // plan.n1
        at = res_hbm.at[pl.ds(pl.multiple_of(base + me1 * piece, 16), piece)]
        return remote(fin.at[c, pl.ds(0, piece)], at, s3_s.at[c, k], s3_r.at[c, k], peer1(plan.offsets1[k])[0])

    def s3_own(c):
        base, size = plan.chunks[c]
        piece = size // plan.n1
        at = res_hbm.at[pl.ds(pl.multiple_of(base + me1 * piece, 16), piece)]
        return pltpu.make_async_copy(fin.at[c, pl.ds(0, piece)], at, loc.at[4 + c])

    def s3_from(c, k):
        base, size = plan.chunks[c]
        piece = size // plan.n1
        device, index = peer1(plan.offsets1[k])
        at = res_hbm.at[pl.ds(pl.multiple_of(base + index * piece, 16), piece)]
        return remote(fin.at[c, pl.ds(0, piece)], at, s3_s.at[c, k], s3_r.at[c, k], device)

    def gather(c):
        piece = plan.chunks[c][1] // plan.n1
        for step in range(1, plan.n2):
            s2_from(c, step).wait_recv()
        total = slot2[c, 0, pl.ds(0, piece)].astype(F32)
        for source in range(1, plan.n2):
            total = total + slot2[c, source, pl.ds(0, piece)].astype(F32)
        fin[c, pl.ds(0, piece)] = (total * factor).astype(BF16)
        for k in range(len(plan.offsets1)):
            s3_copy(c, k).start()
        s3_own(c).start()

    lo_out = pltpu.make_async_copy(lo, lo_hbm.at[0], loc.at[4 + n_chunks])

    def gi_copy(f):
        return pltpu.make_async_copy(gi.at[f], gi_hbm.at[0, f], loc.at[5 + n_chunks + f])

    def grad_in(f):
        pl.when(has_up)(p_copy(f, 0).wait_recv)
        pl.when(has_down)(p_copy(f, 1).wait_recv)
        for r in (0, rows + 1):
            stack(gp, gps, f, r)
        for r, value in spread(gps, wb, f, range(rows + 2)).items():
            gi[f, r - 1] = value.astype(BF16)
        gi_copy(f).start()

    def layer(f):
        mixed = dot(beside([hid[f + 2], hid[f + 1], hid[f]]), wt_ref[...].reshape(3 * ch, ch))
        lo[f] = mixed.astype(BF16).reshape(rows, cols, ch)

    for f in range(frames):
        frame(f)
        if f == frames - 2:
            pl.when(has_next)(h_copy(f).start)
        temporal_grad(f)
        if f == frames - 1:
            scatter(temporal)
        spatial_grad(f)

    for c in range(temporal):
        scatter(c)
    for f in range(frames - 1):
        grad_in(f)
    for c in (temporal, *range(temporal)):
        exchange(c)
    pl.when(has_next)(h_copy(frames - 1).start)
    grad_in(frames - 1)
    layer(frames - 1)
    for c in (temporal, *range(temporal)):
        gather(c)

    @pl.when(has_prev)
    def _():
        for f in (frames - 2, frames - 1):
            h_copy(f).wait_recv()

    for f in range(frames - 1):
        layer(f)
    lo_out.start()

    for f in range(frames):
        pl.when(has_down)(x_copy(f, 0).wait_send)
        pl.when(has_up)(x_copy(f, 1).wait_send)
        pl.when(has_down)(p_copy(f, 0).wait_send)
        pl.when(has_up)(p_copy(f, 1).wait_send)
    for f in range(2):
        pl.when(has_prev)(g_copy(f).wait_send)
    for f in (frames - 2, frames - 1):
        pl.when(has_next)(h_copy(f).wait_send)
    for c in range(n_chunks):
        for k in range(len(plan.offsets1)):
            s1_copy(c, k).wait_send()
        for step in range(1, plan.n2):
            s2_copy(c, step).wait_send()
    for f in range(frames):
        gi_copy(f).wait()
    lo_out.wait()
    for c in (temporal, *range(temporal)):
        s3_own(c).wait()
        for k in range(len(plan.offsets1)):
            s3_copy(c, k).wait_send()
        for k in range(len(plan.offsets1)):
            s3_from(c, k).wait_recv()


def finish(frames, ch, lo, gi, res, lo_hbm, gi_hbm, gs_hbm, gt_hbm, gs, gt, sem):
    copies = []
    for source, target in ((lo, lo_hbm), (gi, gi_hbm)):
        for f in range(frames):
            copies.append(pltpu.make_async_copy(source.at[0, f], target.at[0, f], sem.at[len(copies)]))
    for copy in copies:
        copy.start()
    for i in range(3):
        for j in range(3):
            gs[i, j] = res[pl.ds((3 * j + i) * ch, ch)].astype(F32)
        copies.append(pltpu.make_async_copy(gs.at[i], gs_hbm.at[i], sem.at[len(copies)]))
        copies[-1].start()
    gt[...] = res[pl.ds(9 * ch, 3 * ch)].astype(F32).reshape(3, ch, ch)
    copies.append(pltpu.make_async_copy(gt, gt_hbm, sem.at[len(copies)]))
    copies[-1].start()
    for copy in copies:
        copy.wait()


def per_device(sizes, frames_in, grad_out, w_spatial, w_temporal):
    clips, frames, rows, cols, ch = frames_in.shape
    n_dp, n_tm, n_h = sizes
    assert clips == 1 and n_tm == 4 and frames > 2 and rows > 1
    plan = Plan(sizes, ch)
    assert all(size % (16 * plan.n1) == 0 for _, size in plan.chunks)
    n_chunks, peers1 = len(plan.chunks), len(plan.offsets1)
    factor = 1.0 / math.sqrt(clips * frames * rows * cols * n_dp * n_tm * n_h)
    operands = [
        pltpu.with_memory_space_constraint(a, pltpu.HBM)
        for a in (frames_in, grad_out, w_spatial, w_temporal)
    ]
    any_spec = pl.BlockSpec(memory_space=pl.ANY)
    vmem_spec = pl.BlockSpec(memory_space=pltpu.VMEM)
    hbm_spec = pl.BlockSpec(memory_space=pltpu.HBM)
    dma = pltpu.SemaphoreType.DMA
    block = jax.ShapeDtypeStruct(frames_in.shape, BF16)
    layer_out, grad_in, sums = pl.pallas_call(
        functools.partial(kernel, plan, (frames, rows, cols, ch), factor),
        out_shape=(block, block, jax.ShapeDtypeStruct((12 * ch, ch), BF16)),
        in_specs=[any_spec] * 4,
        out_specs=(any_spec, any_spec, any_spec),
        scratch_shapes=[
            pltpu.VMEM((3, 3, ch, ch), BF16),
            pltpu.VMEM((3, ch, ch), BF16),
            pltpu.VMEM((frames, rows + 2, cols, ch), BF16),
            pltpu.VMEM((frames, rows + 2, cols, 3 * ch), BF16),
            pltpu.VMEM((frames + 2, rows, cols, ch), BF16),
            pltpu.VMEM((frames + 2, rows, cols, ch), BF16),
            pltpu.VMEM((frames, rows + 2, cols, ch), BF16),
            pltpu.VMEM((frames, rows + 2, cols, 3 * ch), BF16),
            pltpu.VMEM((3 * ch, 3 * ch), BF16),
            pltpu.VMEM((3 * ch, 3 * ch), BF16),
            pltpu.VMEM((3 * ch, ch), BF16),
            pltpu.VMEM((frames, rows, cols, ch), F32),
            pltpu.VMEM((frames, rows, cols, ch), F32),
            pltpu.VMEM((12 * ch, ch), F32),
            pltpu.VMEM((12 * ch, ch), BF16),
            pltpu.VMEM((n_chunks, peers1, plan.piece, ch), BF16),
            pltpu.VMEM((n_chunks, plan.n2, plan.piece, ch), BF16),
            pltpu.VMEM((n_chunks, plan.piece, ch), BF16),
            pltpu.VMEM((frames, rows, cols, ch), BF16),
            pltpu.VMEM((frames, rows, cols, ch), BF16),
            dma((5 + n_chunks + frames,)),
            dma((frames, 2)), dma((frames, 2)), dma((2,)), dma((2,)),
            dma((frames,)), dma((frames,)), dma((frames, 2)), dma((frames, 2)),
            dma((n_chunks, peers1)), dma((n_chunks, peers1)),
            dma((n_chunks, plan.n2)), dma((n_chunks, plan.n2)),
            dma((n_chunks, peers1)), dma((n_chunks, peers1)),
        ],
        compiler_params=pltpu.CompilerParams(
            collective_id=0, has_side_effects=True, vmem_limit_bytes=48 << 20
        ),
    )(*operands)
    return pl.pallas_call(
        functools.partial(finish, frames, ch),
        out_shape=(
            block, block,
            jax.ShapeDtypeStruct((3, 3, ch, ch), F32), jax.ShapeDtypeStruct((3, ch, ch), F32),
        ),
        in_specs=[vmem_spec] * 3,
        out_specs=(hbm_spec,) * 4,
        scratch_shapes=[
            pltpu.VMEM((3, 3, ch, ch), F32), pltpu.VMEM((3, ch, ch), F32), dma((2 * frames + 4,)),
        ],
        compiler_params=pltpu.CompilerParams(vmem_limit_bytes=16 << 20),
    )(layer_out, grad_in, sums)


def solution(mesh):
    sizes = (mesh.shape["dp"], mesh.shape["tm"], mesh.shape["height"])
    spec = P("dp", "tm", "height", None, None)
    return jax.shard_map(
        functools.partial(per_device, sizes), mesh=mesh,
        in_specs=(spec, spec, P(), P()), out_specs=(spec, spec, P(), P()), check_vma=False,
    )
```

```python
import functools
import math

import jax
import jax.numpy as jnp
from jax import lax
from jax.experimental import pallas as pl
from jax.experimental.pallas import tpu as pltpu
from jax.sharding import PartitionSpec as P

F32, BF16 = jnp.float32, jnp.bfloat16
MESH = pl.DeviceIdType.MESH
SPATIAL_CHUNKS = 3


def tdot(lhs, rhs):
    return lax.dot_general(lhs, rhs, (((0,), (0,)), ((), ())), preferred_element_type=F32)


def dot(lhs, rhs):
    return jnp.dot(lhs, rhs, preferred_element_type=F32)


class Plan:
    def __init__(self, sizes, ch):
        self.n_dp, self.n_tm, self.n_h = sizes
        self.fold = self.n_dp == 2
        self.n1 = self.n_tm * (self.n_dp if self.fold else 1)
        self.n2 = self.n_h * (1 if self.fold else self.n_dp)
        size = 9 * ch // SPATIAL_CHUNKS
        self.chunks = [(size * k, size) for k in range(SPATIAL_CHUNKS)] + [(9 * ch, 3 * ch)]
        assert all(rows == size for _, rows in self.chunks) and size % (16 * self.n1) == 0
        self.piece = size // self.n1
        self.steps2 = sorted(range(1, self.n2), key=lambda step: abs(2 * step - self.n2))
        self.offsets1 = [
            (a, b, c) for a in ((1, 0) if self.fold else (0,)) for b in (1, 0) for c in (0, 1) if a + b + c
        ]


def kernel(
    plan, dims, factor,
    x_hbm, g_hbm, ws_hbm, wt_hbm,
    lo_hbm, gi_hbm, res_hbm,
    ws_ref, wt_ref, x_ext, xs, g_ext, hid, gp, gps, wf, wb, wtb, pre_s, gh_s, acc, part, slot1, slot2, fin, lo, gi,
    loc, xh_s, xh_r, gh_sem, gh_r, hd_s, hd_r, gp_s, gp_r, s1_s, s1_r, s2_s, s2_r, s3_s, s3_r,
):
    n_dp, n_tm, n_h = plan.n_dp, plan.n_tm, plan.n_h
    frames, rows, cols, ch = dims
    pix = rows * cols
    me_dp, me_tm, me_h = lax.axis_index("dp"), lax.axis_index("tm"), lax.axis_index("height")

    def remote(src, dst, send, recv, device):
        return pltpu.make_async_remote_copy(
            src_ref=src, dst_ref=dst, send_sem=send, recv_sem=recv, device_id=device, device_id_type=MESH,
        )

    def whole(ref, send, recv):
        return remote(ref, ref, send, recv, {"tm": me_tm})

    x_in = pltpu.make_async_copy(x_hbm.at[0], x_ext.at[:, pl.ds(1, rows)], loc.at[0])
    g_in = pltpu.make_async_copy(g_hbm.at[0], g_ext.at[pl.ds(0, frames)], loc.at[1])
    ws_in = pltpu.make_async_copy(ws_hbm, ws_ref, loc.at[2])
    wt_in = pltpu.make_async_copy(wt_hbm, wt_ref, loc.at[3])
    x_in.start()
    ws_in.start()
    wt_in.start()
    g_in.start()

    me_y, me_core = lax.div(me_tm, 2), lax.rem(me_tm, 2)

    def peer1(offset):
        a, b, c = offset
        dp = lax.rem(me_dp + a, 2) if plan.fold else me_dp
        tm = 2 * lax.rem(me_y + b, 2) + lax.rem(me_core + c, 2)
        return {"dp": dp, "tm": tm}, (dp * n_tm + tm if plan.fold else tm)

    me1 = me_dp * n_tm + me_tm if plan.fold else me_tm
    me2 = me_h if plan.fold else me_dp * n_h + me_h

    def peer2(step):
        index = lax.rem(me2 + step, plan.n2)
        if plan.fold:
            return {"height": index}, index
        return {"dp": lax.div(index, n_h), "height": lax.rem(index, n_h)}, index

    barrier = pltpu.get_barrier_semaphore()
    for step in range(1, plan.n2):
        pl.semaphore_signal(barrier, inc=1, device_id=peer2(step)[0], device_id_type=MESH)
    for offset in plan.offsets1:
        pl.semaphore_signal(barrier, inc=1, device_id=peer1(offset)[0], device_id_type=MESH)

    has_up, has_down = me_h > 0, me_h < n_h - 1
    has_prev, has_next = me_tm > 0, me_tm < n_tm - 1
    up, down = lax.rem(me_h + n_h - 1, n_h), lax.rem(me_h + 1, n_h)
    prev, nxt = lax.rem(me_tm + n_tm - 1, n_tm), lax.rem(me_tm + 1, n_tm)

    def x_copy(f, side):
        if side == 0:
            return remote(
                x_hbm.at[0, f, rows - 1], x_ext.at[f, 0], xh_s.at[0], xh_r.at[f, 0], {"height": down}
            )
        return remote(x_hbm.at[0, f, 0], x_ext.at[f, rows + 1], xh_s.at[1], xh_r.at[f, 1], {"height": up})

    def g_copy(f):
        return remote(g_hbm.at[0, f], g_ext.at[frames + f], gh_sem, gh_r.at[f], {"tm": prev})

    def h_copy(f):
        return remote(hid.at[f + 2], hid.at[f + 2 - frames], hd_s, hd_r, {"tm": nxt})

    def p_copy(f, side):
        if side == 0:
            return remote(gp.at[f, rows], gp.at[f, 0], gp_s.at[0], gp_r.at[f, 0], {"height": down})
        return remote(gp.at[f, 1], gp.at[f, rows + 1], gp_s.at[1], gp_r.at[f, 1], {"height": up})

    @pl.when(me_h == 0)
    def _():
        x_ext[:, 0] = jnp.zeros((frames, cols, ch), BF16)
        gp[:, 0] = jnp.zeros((frames, cols, ch), BF16)

    @pl.when(me_h == n_h - 1)
    def _():
        x_ext[:, rows + 1] = jnp.zeros((frames, cols, ch), BF16)
        gp[:, rows + 1] = jnp.zeros((frames, cols, ch), BF16)

    @pl.when(me_tm == 0)
    def _():
        hid[pl.ds(0, 2)] = jnp.zeros((2, rows, cols, ch), BF16)

    @pl.when(me_tm == n_tm - 1)
    def _():
        g_ext[pl.ds(frames, 2)] = jnp.zeros((2, rows, cols, ch), BF16)

    place = lax.broadcasted_iota(jnp.int32, (cols, ch), 0)

    def stack(source, target, f, r):
        value = source[f, r]
        wide = value.astype(F32)
        left = jnp.where(place == 0, 0.0, pltpu.roll(wide, 1, 0))
        right = jnp.where(place == cols - 1, 0.0, pltpu.roll(wide, cols - 1, 0))
        target[f, r, :, pl.ds(0, ch)] = left.astype(BF16)
        target[f, r, :, pl.ds(ch, ch)] = value
        target[f, r, :, pl.ds(2 * ch, ch)] = right.astype(BF16)

    def spread(source, weights, f, sources):
        sums = {}
        for s in sources:
            first, last = max(1, s - 1), min(rows, s + 1)
            at = first - s + 1
            wide = dot(source[f, s], weights[:, at * ch : (at + last - first + 1) * ch])
            for r in range(first, last + 1):
                term = wide[:, (r - first) * ch : (r - first + 1) * ch]
                sums[r] = sums[r] + term if r in sums else term
        return sums

    def beside(parts):
        return jnp.concatenate([p.reshape(pix, ch) for p in parts], axis=1)

    x_in.wait()

    @pl.loop(0, frames)
    def _(f):
        for r in range(1, rows + 1):
            stack(x_ext, xs, f, r)

    pl.semaphore_wait(barrier, plan.n2 - 1 + len(plan.offsets1))
    for f in range(frames):
        pl.when(has_down)(x_copy(f, 0).start)
        pl.when(has_up)(x_copy(f, 1).start)
    for f in range(2):
        pl.when(has_prev)(g_copy(f).start)

    ws_in.wait()
    wt_in.wait()
    for i in range(3):
        wf[:, pl.ds((2 - i) * ch, ch)] = ws_ref[i].reshape(3 * ch, ch)
        for j in range(3):
            wb[pl.ds((2 - j) * ch, ch), pl.ds(i * ch, ch)] = ws_ref[i, j].T
        wtb[pl.ds(i * ch, ch)] = wt_ref[i].T

    @pl.loop(0, frames)
    def _(f):
        for r, value in spread(xs, wf, f, range(1, rows + 1)).items():
            pre_s[f, r - 1] = value

    g_in.wait()
    for f in range(frames):
        near = min(3, frames - f)
        value = dot(beside([g_ext[f + k] for k in range(near)]), wtb[pl.ds(0, near * ch)])
        gh_s[f] = value.reshape(rows, cols, ch)

    acc[...] = jnp.zeros(acc.shape, F32)

    def frame(f):
        pl.when(has_up)(x_copy(f, 0).wait_recv)
        pl.when(has_down)(x_copy(f, 1).wait_recv)
        near = min(3, frames - f)
        if near < 3:
            pl.when(has_next)(g_copy(2 - near).wait_recv)
        for r in (0, rows + 1):
            stack(x_ext, xs, f, r)
        edge = spread(xs, wf, f, (0, rows + 1))
        far = None
        if near < 3:
            far = dot(beside([g_ext[f + k] for k in range(near, 3)]), wtb[pl.ds(near * ch, (3 - near) * ch)])
            far = far.reshape(rows, cols, ch)
        for r in range(1, rows + 1):
            pre = pre_s[f, r - 1]
            if r in edge:
                pre = pre + edge[r]
            sigma = jax.nn.sigmoid(pre)
            hid[f + 2, r - 1] = (pre * sigma).astype(BF16)
            grad_hidden = gh_s[f, r - 1]
            if far is not None:
                grad_hidden = grad_hidden + far[r - 1]
            grad_pre = grad_hidden * sigma * (1.0 + pre * (1.0 - sigma))
            gp[f, r] = grad_pre.astype(BF16)
            stack(gp, gps, f, r)
        pl.when(has_down)(p_copy(f, 0).start)
        pl.when(has_up)(p_copy(f, 1).start)

    def temporal_grad(f):
        term = tdot(hid[f + 2].reshape(pix, ch), beside([g_ext[f + k] for k in range(3)]))
        for k in range(3):
            acc[pl.ds((9 + k) * ch, ch)] += term[:, k * ch : (k + 1) * ch]

    def spatial_grad(f):
        term = tdot(
            beside([x_ext[f, pl.ds(i, rows)] for i in range(3)]),
            gps[f, pl.ds(1, rows)].reshape(pix, 3 * ch),
        )
        for j in range(3):
            acc[pl.ds(3 * j * ch, 3 * ch)] += term[:, (2 - j) * ch : (3 - j) * ch]

    n_chunks = len(plan.chunks)
    temporal = n_chunks - 1

    def s1_copy(c, k):
        base, size = plan.chunks[c]
        piece = size // plan.n1
        device, index = peer1(plan.offsets1[k])
        return remote(
            part.at[pl.ds(pl.multiple_of(base + index * piece, 16), piece)],
            slot1.at[c, k], s1_s, s1_r.at[c], device,
        )

    def scatter(c):
        base, size = plan.chunks[c]
        part[pl.ds(base, size)] = acc[pl.ds(base, size)].astype(BF16)
        for k in range(len(plan.offsets1)):
            s1_copy(c, k).start()

    def s2_copy(c, step):
        device, _ = peer2(step)
        at = slot2.at[c, me2]
        return remote(at, at, s2_s, s2_r.at[c], device)

    def exchange(c):
        base, size = plan.chunks[c]
        piece = size // plan.n1
        total = acc[pl.ds(pl.multiple_of(base + me1 * piece, 16), piece)]
        whole(slot1.at[c], s1_s, s1_r.at[c]).wait_recv()
        for k in range(len(plan.offsets1)):
            total = total + slot1[c, k].astype(F32)
        slot2[c, me2] = total.astype(BF16)
        for step in plan.steps2:
            s2_copy(c, step).start()

    def s3_copy(c, k):
        base, size = plan.chunks[c]
        piece = size // plan.n1
        at = res_hbm.at[pl.ds(pl.multiple_of(base + me1 * piece, 16), piece)]
        return remote(fin.at[c], at, s3_s, s3_r.at[c], peer1(plan.offsets1[k])[0])

    def s3_own(c):
        base, size = plan.chunks[c]
        piece = size // plan.n1
        at = res_hbm.at[pl.ds(pl.multiple_of(base + me1 * piece, 16), piece)]
        return pltpu.make_async_copy(fin.at[c], at, loc.at[6])

    def gather(c):
        whole(slot2.at[c, pl.ds(0, plan.n2 - 1)], s2_s, s2_r.at[c]).wait_recv()
        total = slot2[c, 0].astype(F32)
        for source in range(1, plan.n2):
            total = total + slot2[c, source].astype(F32)
        fin[c] = (total * factor).astype(BF16)
        for k in range(len(plan.offsets1)):
            s3_copy(c, k).start()
        s3_own(c).start()

    lo_out = pltpu.make_async_copy(lo, lo_hbm.at[0], loc.at[4])

    def gi_copy(f):
        return pltpu.make_async_copy(gi.at[f], gi_hbm.at[0, f], loc.at[5])

    def grad_in(f):
        pl.when(has_up)(p_copy(f, 0).wait_recv)
        pl.when(has_down)(p_copy(f, 1).wait_recv)
        for r in (0, rows + 1):
            stack(gp, gps, f, r)
        for r, value in spread(gps, wb, f, range(rows + 2)).items():
            gi[f, r - 1] = value.astype(BF16)
        gi_copy(f).start()

    def layer(f):
        mixed = dot(beside([hid[f + 2], hid[f + 1], hid[f]]), wt_ref[...].reshape(3 * ch, ch))
        lo[f] = mixed.astype(BF16).reshape(rows, cols, ch)

    for f in range(frames):
        frame(f)
        if f == frames - 2:
            pl.when(has_next)(h_copy(f).start)
        temporal_grad(f)
        if f == frames - 1:
            scatter(temporal)
        spatial_grad(f)

    for c in range(temporal):
        scatter(c)
    for f in range(frames - 1):
        grad_in(f)
    for c in (temporal, *range(temporal)):
        exchange(c)
    pl.when(has_next)(h_copy(frames - 1).start)
    grad_in(frames - 1)
    layer(frames - 1)
    for c in (temporal, *range(temporal)):
        gather(c)

    pl.when(has_prev)(whole(hid.at[pl.ds(0, 2)], hd_s, hd_r).wait_recv)

    for f in range(frames - 1):
        layer(f)
    lo_out.start()

    pl.when(has_down)(whole(x_ext.at[:, 0], xh_s.at[0], xh_r.at[0, 0]).wait_send)
    pl.when(has_up)(whole(x_ext.at[:, 0], xh_s.at[1], xh_r.at[0, 0]).wait_send)
    pl.when(has_down)(whole(gp.at[:, 0], gp_s.at[0], gp_r.at[0, 0]).wait_send)
    pl.when(has_up)(whole(gp.at[:, 0], gp_s.at[1], gp_r.at[0, 0]).wait_send)
    pl.when(has_prev)(whole(g_ext.at[pl.ds(0, 2)], gh_sem, gh_r.at[0]).wait_send)
    pl.when(has_next)(whole(hid.at[pl.ds(0, 2)], hd_s, hd_r).wait_send)
    whole(slot1, s1_s, s1_r.at[0]).wait_send()
    whole(slot2.at[:, pl.ds(0, plan.n2 - 1)], s2_s, s2_r.at[0]).wait_send()
    pltpu.make_async_copy(gi, gi_hbm.at[0], loc.at[5]).wait()
    lo_out.wait()
    pltpu.make_async_copy(fin, fin, loc.at[6]).wait()
    for c in (temporal, *range(temporal)):
        whole(slot1.at[c], s3_s, s3_r.at[c]).wait_recv()
    whole(slot1, s3_s, s3_r.at[0]).wait_send()


def finish(frames, ch, lo, gi, res, lo_hbm, gi_hbm, gs_hbm, gt_hbm, gs, gt, sem):
    copies = []
    for source, target in ((lo, lo_hbm), (gi, gi_hbm)):
        for f in range(frames):
            copies.append(pltpu.make_async_copy(source.at[0, f], target.at[0, f], sem.at[len(copies)]))
    for copy in copies:
        copy.start()
    for i in range(3):
        for j in range(3):
            gs[i, j] = res[pl.ds((3 * j + i) * ch, ch)].astype(F32)
        copies.append(pltpu.make_async_copy(gs.at[i], gs_hbm.at[i], sem.at[len(copies)]))
        copies[-1].start()
    gt[...] = res[pl.ds(9 * ch, 3 * ch)].astype(F32).reshape(3, ch, ch)
    copies.append(pltpu.make_async_copy(gt, gt_hbm, sem.at[len(copies)]))
    copies[-1].start()
    for copy in copies:
        copy.wait()


def per_device(sizes, frames_in, grad_out, w_spatial, w_temporal):
    clips, frames, rows, cols, ch = frames_in.shape
    n_dp, n_tm, n_h = sizes
    assert clips == 1 and n_tm == 4 and frames > 2 and rows > 1
    plan = Plan(sizes, ch)
    n_chunks, peers1 = len(plan.chunks), len(plan.offsets1)
    factor = 1.0 / math.sqrt(clips * frames * rows * cols * n_dp * n_tm * n_h)
    operands = [
        pltpu.with_memory_space_constraint(a, pltpu.HBM)
        for a in (frames_in, grad_out, w_spatial, w_temporal)
    ]
    any_spec = pl.BlockSpec(memory_space=pl.ANY)
    vmem_spec = pl.BlockSpec(memory_space=pltpu.VMEM)
    hbm_spec = pl.BlockSpec(memory_space=pltpu.HBM)
    dma = pltpu.SemaphoreType.DMA
    block = jax.ShapeDtypeStruct(frames_in.shape, BF16)
    layer_out, grad_in, sums = pl.pallas_call(
        functools.partial(kernel, plan, (frames, rows, cols, ch), factor),
        out_shape=(block, block, jax.ShapeDtypeStruct((12 * ch, ch), BF16)),
        in_specs=[any_spec] * 4,
        out_specs=(any_spec, any_spec, any_spec),
        scratch_shapes=[
            pltpu.VMEM((3, 3, ch, ch), BF16),
            pltpu.VMEM((3, ch, ch), BF16),
            pltpu.VMEM((frames, rows + 2, cols, ch), BF16),
            pltpu.VMEM((frames, rows + 2, cols, 3 * ch), BF16),
            pltpu.VMEM((frames + 2, rows, cols, ch), BF16),
            pltpu.VMEM((frames + 2, rows, cols, ch), BF16),
            pltpu.VMEM((frames, rows + 2, cols, ch), BF16),
            pltpu.VMEM((frames, rows + 2, cols, 3 * ch), BF16),
            pltpu.VMEM((3 * ch, 3 * ch), BF16),
            pltpu.VMEM((3 * ch, 3 * ch), BF16),
            pltpu.VMEM((3 * ch, ch), BF16),
            pltpu.VMEM((frames, rows, cols, ch), F32),
            pltpu.VMEM((frames, rows, cols, ch), F32),
            pltpu.VMEM((12 * ch, ch), F32),
            pltpu.VMEM((12 * ch, ch), BF16),
            pltpu.VMEM((n_chunks, peers1, plan.piece, ch), BF16),
            pltpu.VMEM((n_chunks, plan.n2, plan.piece, ch), BF16),
            pltpu.VMEM((n_chunks, plan.piece, ch), BF16),
            pltpu.VMEM((frames, rows, cols, ch), BF16),
            pltpu.VMEM((frames, rows, cols, ch), BF16),
            dma((7,)),
            dma((2,)), dma((frames, 2)), dma, dma((2,)), dma, dma, dma((2,)), dma((frames, 2)),
            dma, dma((n_chunks,)), dma, dma((n_chunks,)), dma, dma((n_chunks,)),
        ],
        compiler_params=pltpu.CompilerParams(
            collective_id=0, has_side_effects=True, vmem_limit_bytes=48 << 20
        ),
    )(*operands)
    return pl.pallas_call(
        functools.partial(finish, frames, ch),
        out_shape=(
            block, block,
            jax.ShapeDtypeStruct((3, 3, ch, ch), F32), jax.ShapeDtypeStruct((3, ch, ch), F32),
        ),
        in_specs=[vmem_spec] * 3,
        out_specs=(hbm_spec,) * 4,
        scratch_shapes=[
            pltpu.VMEM((3, 3, ch, ch), F32), pltpu.VMEM((3, ch, ch), F32), dma((2 * frames + 4,)),
        ],
        compiler_params=pltpu.CompilerParams(vmem_limit_bytes=16 << 20),
    )(layer_out, grad_in, sums)


def solution(mesh):
    sizes = (mesh.shape["dp"], mesh.shape["tm"], mesh.shape["height"])
    spec = P("dp", "tm", "height", None, None)
    return jax.shard_map(
        functools.partial(per_device, sizes), mesh=mesh,
        in_specs=(spec, spec, P(), P()), out_specs=(spec, spec, P(), P()), check_vma=False,
    )
```

```python
import functools
import math

import jax
import jax.numpy as jnp
from jax import lax
from jax.experimental import pallas as pl
from jax.experimental.pallas import tpu as pltpu
from jax.sharding import PartitionSpec as P

F32, BF16 = jnp.float32, jnp.bfloat16
MESH = pl.DeviceIdType.MESH
SPATIAL_CHUNKS = 3


def tdot(lhs, rhs):
    return lax.dot_general(lhs, rhs, (((0,), (0,)), ((), ())), preferred_element_type=F32)


def dot(lhs, rhs):
    return jnp.dot(lhs, rhs, preferred_element_type=F32)


class Plan:
    def __init__(self, sizes, ch):
        self.n_dp, self.n_tm, self.n_h = sizes
        self.fold = self.n_dp == 2
        self.n1 = self.n_tm * (self.n_dp if self.fold else 1)
        self.n2 = self.n_h * (1 if self.fold else self.n_dp)
        size = 9 * ch // SPATIAL_CHUNKS
        self.chunks = [(size * k, size) for k in range(SPATIAL_CHUNKS)] + [(9 * ch, 3 * ch)]
        assert all(rows == size for _, rows in self.chunks) and size % (16 * self.n1) == 0
        self.piece = size // self.n1
        self.steps2 = sorted(range(1, self.n2), key=lambda step: abs(2 * step - self.n2))
        self.offsets1 = [
            (a, b, c) for a in ((1, 0) if self.fold else (0,)) for b in (1, 0) for c in (0, 1) if a + b + c
        ]


def kernel(
    plan, dims, factor,
    x_hbm, g_hbm, ws_hbm, wt_hbm,
    lo_hbm, gi_hbm, res_hbm,
    ws_ref, wt_ref, x_ext, xs, g_ext, hid, gp, gps, wf, wb, wtb, pre_s, gh_s, acc, part, slot1, slot2, fin, lo, gi,
    loc, xh_s, xh_r, gh_sem, gh_r, hd_s, hd_r, gp_s, gp_r, s1_s, s1_r, s2_s, s2_r, s3_s, s3_r,
):
    n_dp, n_tm, n_h = plan.n_dp, plan.n_tm, plan.n_h
    frames, rows, cols, ch = dims
    pix = rows * cols
    me_dp, me_tm, me_h = lax.axis_index("dp"), lax.axis_index("tm"), lax.axis_index("height")

    def remote(src, dst, send, recv, device):
        return pltpu.make_async_remote_copy(
            src_ref=src, dst_ref=dst, send_sem=send, recv_sem=recv, device_id=device, device_id_type=MESH,
        )

    def whole(ref, send, recv):
        return remote(ref, ref, send, recv, {"tm": me_tm})

    x_in = pltpu.make_async_copy(x_hbm.at[0], x_ext.at[:, pl.ds(1, rows)], loc.at[0])
    g_in = pltpu.make_async_copy(g_hbm.at[0], g_ext.at[pl.ds(0, frames)], loc.at[1])
    ws_in = pltpu.make_async_copy(ws_hbm, ws_ref, loc.at[2])
    wt_in = pltpu.make_async_copy(wt_hbm, wt_ref, loc.at[3])
    x_in.start()
    ws_in.start()
    wt_in.start()
    g_in.start()

    me_y, me_core = lax.div(me_tm, 2), lax.rem(me_tm, 2)

    def peer1(offset):
        a, b, c = offset
        dp = lax.rem(me_dp + a, 2) if plan.fold else me_dp
        tm = 2 * lax.rem(me_y + b, 2) + lax.rem(me_core + c, 2)
        return {"dp": dp, "tm": tm}, (dp * n_tm + tm if plan.fold else tm)

    me1 = me_dp * n_tm + me_tm if plan.fold else me_tm
    me2 = me_h if plan.fold else me_dp * n_h + me_h

    def peer2(step):
        index = lax.rem(me2 + step, plan.n2)
        if plan.fold:
            return {"height": index}, index
        return {"dp": lax.div(index, n_h), "height": lax.rem(index, n_h)}, index

    barrier = pltpu.get_barrier_semaphore()
    for step in range(1, plan.n2):
        pl.semaphore_signal(barrier, inc=1, device_id=peer2(step)[0], device_id_type=MESH)
    for offset in plan.offsets1:
        pl.semaphore_signal(barrier, inc=1, device_id=peer1(offset)[0], device_id_type=MESH)

    has_up, has_down = me_h > 0, me_h < n_h - 1
    has_prev, has_next = me_tm > 0, me_tm < n_tm - 1
    up, down = lax.rem(me_h + n_h - 1, n_h), lax.rem(me_h + 1, n_h)
    prev, nxt = lax.rem(me_tm + n_tm - 1, n_tm), lax.rem(me_tm + 1, n_tm)

    def x_copy(f, side):
        if side == 0:
            return remote(
                x_hbm.at[0, f, rows - 1], x_ext.at[f, 0], xh_s.at[0], xh_r.at[f, 0], {"height": down}
            )
        return remote(x_hbm.at[0, f, 0], x_ext.at[f, rows + 1], xh_s.at[1], xh_r.at[f, 1], {"height": up})

    def g_copy(f):
        return remote(g_hbm.at[0, f], g_ext.at[frames + f], gh_sem, gh_r.at[f], {"tm": prev})

    def h_copy(f):
        return remote(hid.at[f + 2], hid.at[f + 2 - frames], hd_s, hd_r, {"tm": nxt})

    def p_copy(f, side):
        if side == 0:
            return remote(gp.at[f, rows], gp.at[f, 0], gp_s.at[0], gp_r.at[f, 0], {"height": down})
        return remote(gp.at[f, 1], gp.at[f, rows + 1], gp_s.at[1], gp_r.at[f, 1], {"height": up})

    @pl.when(me_h == 0)
    def _():
        x_ext[:, 0] = jnp.zeros((frames, cols, ch), BF16)
        gp[:, 0] = jnp.zeros((frames, cols, ch), BF16)

    @pl.when(me_h == n_h - 1)
    def _():
        x_ext[:, rows + 1] = jnp.zeros((frames, cols, ch), BF16)
        gp[:, rows + 1] = jnp.zeros((frames, cols, ch), BF16)

    @pl.when(me_tm == 0)
    def _():
        hid[pl.ds(0, 2)] = jnp.zeros((2, rows, cols, ch), BF16)

    @pl.when(me_tm == n_tm - 1)
    def _():
        g_ext[pl.ds(frames, 2)] = jnp.zeros((2, rows, cols, ch), BF16)

    place = lax.broadcasted_iota(jnp.int32, (cols, ch), 0)

    def stack(source, target, f, r):
        value = source[f, r]
        wide = value.astype(F32)
        left = jnp.where(place == 0, 0.0, pltpu.roll(wide, 1, 0))
        right = jnp.where(place == cols - 1, 0.0, pltpu.roll(wide, cols - 1, 0))
        target[f, r, :, pl.ds(0, ch)] = left.astype(BF16)
        target[f, r, :, pl.ds(ch, ch)] = value
        target[f, r, :, pl.ds(2 * ch, ch)] = right.astype(BF16)

    def spread(source, weights, f, sources):
        sums = {}
        for s in sources:
            first, last = max(1, s - 1), min(rows, s + 1)
            at = first - s + 1
            wide = dot(source[f, s], weights[:, at * ch : (at + last - first + 1) * ch])
            for r in range(first, last + 1):
                term = wide[:, (r - first) * ch : (r - first + 1) * ch]
                sums[r] = sums[r] + term if r in sums else term
        return sums

    def beside(parts):
        return jnp.concatenate([p.reshape(pix, ch) for p in parts], axis=1)

    x_in.wait()

    @pl.loop(0, frames)
    def _(f):
        for r in range(1, rows + 1):
            stack(x_ext, xs, f, r)

    pl.semaphore_wait(barrier, plan.n2 - 1 + len(plan.offsets1))
    for f in range(frames):
        pl.when(has_down)(x_copy(f, 0).start)
        pl.when(has_up)(x_copy(f, 1).start)
    for f in range(2):
        pl.when(has_prev)(g_copy(f).start)

    ws_in.wait()
    wt_in.wait()
    for i in range(3):
        wf[:, pl.ds((2 - i) * ch, ch)] = ws_ref[i].reshape(3 * ch, ch)
        for j in range(3):
            wb[pl.ds((2 - j) * ch, ch), pl.ds(i * ch, ch)] = ws_ref[i, j].T
        wtb[pl.ds(i * ch, ch)] = wt_ref[i].T

    @pl.loop(0, frames)
    def _(f):
        for r, value in spread(xs, wf, f, range(1, rows + 1)).items():
            pre_s[f, r - 1] = value

    g_in.wait()
    for f in range(frames):
        near = min(3, frames - f)
        value = dot(beside([g_ext[f + k] for k in range(near)]), wtb[pl.ds(0, near * ch)])
        gh_s[f] = value.reshape(rows, cols, ch)

    acc[...] = jnp.zeros(acc.shape, F32)

    def activate(f):
        pl.when(has_up)(x_copy(f, 0).wait_recv)
        pl.when(has_down)(x_copy(f, 1).wait_recv)
        for r in (0, rows + 1):
            stack(x_ext, xs, f, r)
        edge = spread(xs, wf, f, (0, rows + 1))
        for r in range(1, rows + 1):
            pre = pre_s[f, r - 1]
            if r in edge:
                pre = pre + edge[r]
            sigma = jax.nn.sigmoid(pre)
            hid[f + 2, r - 1] = (pre * sigma).astype(BF16)
            pre_s[f, r - 1] = sigma * (1.0 + pre * (1.0 - sigma))

    def back(f):
        near = min(3, frames - f)
        far = None
        if near < 3:
            far = dot(beside([g_ext[f + k] for k in range(near, 3)]), wtb[pl.ds(near * ch, (3 - near) * ch)])
            far = far.reshape(rows, cols, ch)
        for r in range(1, rows + 1):
            grad_hidden = gh_s[f, r - 1]
            if far is not None:
                grad_hidden = grad_hidden + far[r - 1]
            gp[f, r] = (grad_hidden * pre_s[f, r - 1]).astype(BF16)
            stack(gp, gps, f, r)

    def p_start(f):
        pl.when(has_down)(p_copy(f, 0).start)
        pl.when(has_up)(p_copy(f, 1).start)

    def temporal_grad(f):
        term = tdot(hid[f + 2].reshape(pix, ch), beside([g_ext[f + k] for k in range(3)]))
        for k in range(3):
            acc[pl.ds((9 + k) * ch, ch)] += term[:, k * ch : (k + 1) * ch]

    def spatial_grad(f):
        term = tdot(
            beside([x_ext[f, pl.ds(i, rows)] for i in range(3)]),
            gps[f, pl.ds(1, rows)].reshape(pix, 3 * ch),
        )
        for j in range(3):
            acc[pl.ds(3 * j * ch, 3 * ch)] += term[:, (2 - j) * ch : (3 - j) * ch]

    n_chunks = len(plan.chunks)
    temporal = n_chunks - 1

    def s1_copy(c, k):
        base, size = plan.chunks[c]
        piece = size // plan.n1
        device, index = peer1(plan.offsets1[k])
        return remote(
            part.at[pl.ds(pl.multiple_of(base + index * piece, 16), piece)],
            slot1.at[c, k], s1_s, s1_r.at[c], device,
        )

    def scatter(c):
        base, size = plan.chunks[c]
        part[pl.ds(base, size)] = acc[pl.ds(base, size)].astype(BF16)
        for k in range(len(plan.offsets1)):
            s1_copy(c, k).start()

    def s2_copy(c, step):
        device, _ = peer2(step)
        at = slot2.at[c, me2]
        return remote(at, at, s2_s, s2_r.at[c], device)

    def exchange(c):
        base, size = plan.chunks[c]
        piece = size // plan.n1
        total = acc[pl.ds(pl.multiple_of(base + me1 * piece, 16), piece)]
        whole(slot1.at[c], s1_s, s1_r.at[c]).wait_recv()
        for k in range(len(plan.offsets1)):
            total = total + slot1[c, k].astype(F32)
        slot2[c, me2] = total.astype(BF16)
        for step in plan.steps2:
            s2_copy(c, step).start()

    def s3_copy(c, k):
        base, size = plan.chunks[c]
        piece = size // plan.n1
        at = res_hbm.at[pl.ds(pl.multiple_of(base + me1 * piece, 16), piece)]
        return remote(fin.at[c], at, s3_s, s3_r.at[c], peer1(plan.offsets1[k])[0])

    def s3_own(c):
        base, size = plan.chunks[c]
        piece = size // plan.n1
        at = res_hbm.at[pl.ds(pl.multiple_of(base + me1 * piece, 16), piece)]
        return pltpu.make_async_copy(fin.at[c], at, loc.at[6])

    def gather(c):
        whole(slot2.at[c, pl.ds(0, plan.n2 - 1)], s2_s, s2_r.at[c]).wait_recv()
        total = slot2[c, 0].astype(F32)
        for source in range(1, plan.n2):
            total = total + slot2[c, source].astype(F32)
        fin[c] = (total * factor).astype(BF16)
        for k in range(len(plan.offsets1)):
            s3_copy(c, k).start()
        s3_own(c).start()

    lo_out = pltpu.make_async_copy(lo, lo_hbm.at[0], loc.at[4])

    def gi_copy(f):
        return pltpu.make_async_copy(gi.at[f], gi_hbm.at[0, f], loc.at[5])

    def grad_in(f):
        pl.when(has_up)(p_copy(f, 0).wait_recv)
        pl.when(has_down)(p_copy(f, 1).wait_recv)
        for r in (0, rows + 1):
            stack(gp, gps, f, r)
        for r, value in spread(gps, wb, f, range(rows + 2)).items():
            gi[f, r - 1] = value.astype(BF16)
        gi_copy(f).start()

    def layer(f):
        mixed = dot(beside([hid[f + 2], hid[f + 1], hid[f]]), wt_ref[...].reshape(3 * ch, ch))
        lo[f] = mixed.astype(BF16).reshape(rows, cols, ch)

    for f in range(frames):
        activate(f)
        if f == frames - 2:
            pl.when(has_next)(h_copy(f).start)
        if f + 2 >= frames:
            pl.when(has_next)(g_copy(f + 2 - frames).wait_recv)
        back(f)
        if f < frames - 1:
            p_start(f)
        temporal_grad(f)
        if f == frames - 1:
            scatter(temporal)
        spatial_grad(f)

    for c in range(temporal):
        scatter(c)
    for f in range(frames - 1):
        grad_in(f)
    for c in (temporal, *range(temporal)):
        exchange(c)
    p_start(frames - 1)
    pl.when(has_next)(h_copy(frames - 1).start)
    layer(frames - 1)
    for c in (temporal, *range(temporal)):
        gather(c)
    grad_in(frames - 1)

    pl.when(has_prev)(whole(hid.at[pl.ds(0, 2)], hd_s, hd_r).wait_recv)

    for f in range(frames - 1):
        layer(f)
    lo_out.start()

    pl.when(has_down)(whole(x_ext.at[:, 0], xh_s.at[0], xh_r.at[0, 0]).wait_send)
    pl.when(has_up)(whole(x_ext.at[:, 0], xh_s.at[1], xh_r.at[0, 0]).wait_send)
    pl.when(has_down)(whole(gp.at[:, 0], gp_s.at[0], gp_r.at[0, 0]).wait_send)
    pl.when(has_up)(whole(gp.at[:, 0], gp_s.at[1], gp_r.at[0, 0]).wait_send)
    pl.when(has_prev)(whole(g_ext.at[pl.ds(0, 2)], gh_sem, gh_r.at[0]).wait_send)
    pl.when(has_next)(whole(hid.at[pl.ds(0, 2)], hd_s, hd_r).wait_send)
    whole(slot1, s1_s, s1_r.at[0]).wait_send()
    whole(slot2.at[:, pl.ds(0, plan.n2 - 1)], s2_s, s2_r.at[0]).wait_send()
    pltpu.make_async_copy(gi, gi_hbm.at[0], loc.at[5]).wait()
    lo_out.wait()
    pltpu.make_async_copy(fin, fin, loc.at[6]).wait()
    for c in (temporal, *range(temporal)):
        whole(slot1.at[c], s3_s, s3_r.at[c]).wait_recv()
    whole(slot1, s3_s, s3_r.at[0]).wait_send()


def finish(frames, ch, lo, gi, res, lo_hbm, gi_hbm, gs_hbm, gt_hbm, gs, gt, sem):
    copies = []
    for source, target in ((lo, lo_hbm), (gi, gi_hbm)):
        for f in range(frames):
            copies.append(pltpu.make_async_copy(source.at[0, f], target.at[0, f], sem.at[len(copies)]))
    for copy in copies:
        copy.start()
    for i in range(3):
        for j in range(3):
            gs[i, j] = res[pl.ds((3 * j + i) * ch, ch)].astype(F32)
        copies.append(pltpu.make_async_copy(gs.at[i], gs_hbm.at[i], sem.at[len(copies)]))
        copies[-1].start()
    gt[...] = res[pl.ds(9 * ch, 3 * ch)].astype(F32).reshape(3, ch, ch)
    copies.append(pltpu.make_async_copy(gt, gt_hbm, sem.at[len(copies)]))
    copies[-1].start()
    for copy in copies:
        copy.wait()


def per_device(sizes, frames_in, grad_out, w_spatial, w_temporal):
    clips, frames, rows, cols, ch = frames_in.shape
    n_dp, n_tm, n_h = sizes
    assert clips == 1 and n_tm == 4 and frames > 2 and rows > 1
    plan = Plan(sizes, ch)
    n_chunks, peers1 = len(plan.chunks), len(plan.offsets1)
    factor = 1.0 / math.sqrt(clips * frames * rows * cols * n_dp * n_tm * n_h)
    operands = [
        pltpu.with_memory_space_constraint(a, pltpu.HBM)
        for a in (frames_in, grad_out, w_spatial, w_temporal)
    ]
    any_spec = pl.BlockSpec(memory_space=pl.ANY)
    vmem_spec = pl.BlockSpec(memory_space=pltpu.VMEM)
    hbm_spec = pl.BlockSpec(memory_space=pltpu.HBM)
    dma = pltpu.SemaphoreType.DMA
    block = jax.ShapeDtypeStruct(frames_in.shape, BF16)
    layer_out, grad_in, sums = pl.pallas_call(
        functools.partial(kernel, plan, (frames, rows, cols, ch), factor),
        out_shape=(block, block, jax.ShapeDtypeStruct((12 * ch, ch), BF16)),
        in_specs=[any_spec] * 4,
        out_specs=(any_spec, any_spec, any_spec),
        scratch_shapes=[
            pltpu.VMEM((3, 3, ch, ch), BF16),
            pltpu.VMEM((3, ch, ch), BF16),
            pltpu.VMEM((frames, rows + 2, cols, ch), BF16),
            pltpu.VMEM((frames, rows + 2, cols, 3 * ch), BF16),
            pltpu.VMEM((frames + 2, rows, cols, ch), BF16),
            pltpu.VMEM((frames + 2, rows, cols, ch), BF16),
            pltpu.VMEM((frames, rows + 2, cols, ch), BF16),
            pltpu.VMEM((frames, rows + 2, cols, 3 * ch), BF16),
            pltpu.VMEM((3 * ch, 3 * ch), BF16),
            pltpu.VMEM((3 * ch, 3 * ch), BF16),
            pltpu.VMEM((3 * ch, ch), BF16),
            pltpu.VMEM((frames, rows, cols, ch), F32),
            pltpu.VMEM((frames, rows, cols, ch), F32),
            pltpu.VMEM((12 * ch, ch), F32),
            pltpu.VMEM((12 * ch, ch), BF16),
            pltpu.VMEM((n_chunks, peers1, plan.piece, ch), BF16),
            pltpu.VMEM((n_chunks, plan.n2, plan.piece, ch), BF16),
            pltpu.VMEM((n_chunks, plan.piece, ch), BF16),
            pltpu.VMEM((frames, rows, cols, ch), BF16),
            pltpu.VMEM((frames, rows, cols, ch), BF16),
            dma((7,)),
            dma((2,)), dma((frames, 2)), dma, dma((2,)), dma, dma, dma((2,)), dma((frames, 2)),
            dma, dma((n_chunks,)), dma, dma((n_chunks,)), dma, dma((n_chunks,)),
        ],
        compiler_params=pltpu.CompilerParams(
            collective_id=0, has_side_effects=True, vmem_limit_bytes=48 << 20
        ),
    )(*operands)
    return pl.pallas_call(
        functools.partial(finish, frames, ch),
        out_shape=(
            block, block,
            jax.ShapeDtypeStruct((3, 3, ch, ch), F32), jax.ShapeDtypeStruct((3, ch, ch), F32),
        ),
        in_specs=[vmem_spec] * 3,
        out_specs=(hbm_spec,) * 4,
        scratch_shapes=[
            pltpu.VMEM((3, 3, ch, ch), F32), pltpu.VMEM((3, ch, ch), F32), dma((2 * frames + 4,)),
        ],
        compiler_params=pltpu.CompilerParams(vmem_limit_bytes=16 << 20),
    )(layer_out, grad_in, sums)


def solution(mesh):
    sizes = (mesh.shape["dp"], mesh.shape["tm"], mesh.shape["height"])
    spec = P("dp", "tm", "height", None, None)
    return jax.shard_map(
        functools.partial(per_device, sizes), mesh=mesh,
        in_specs=(spec, spec, P(), P()), out_specs=(spec, spec, P(), P()), check_vma=False,
    )
```

```python
import functools
import math

import jax
import jax.numpy as jnp
from jax import lax
from jax.experimental import pallas as pl
from jax.experimental.pallas import tpu as pltpu
from jax.sharding import PartitionSpec as P

F32, BF16 = jnp.float32, jnp.bfloat16
MESH = pl.DeviceIdType.MESH
SPATIAL_CHUNKS = 3


def tdot(lhs, rhs):
    return lax.dot_general(lhs, rhs, (((0,), (0,)), ((), ())), preferred_element_type=F32)


def dot(lhs, rhs):
    return jnp.dot(lhs, rhs, preferred_element_type=F32)


class Plan:
    def __init__(self, sizes, ch):
        self.n_dp, self.n_tm, self.n_h = sizes
        self.fold = self.n_dp == 2
        self.n1 = self.n_tm * (self.n_dp if self.fold else 1)
        self.n2 = self.n_h * (1 if self.fold else self.n_dp)
        size = 9 * ch // SPATIAL_CHUNKS
        self.chunks = [(size * k, size) for k in range(SPATIAL_CHUNKS)] + [(9 * ch, 3 * ch)]
        assert all(rows == size for _, rows in self.chunks) and size % (16 * self.n1) == 0
        self.piece = size // self.n1
        self.steps2 = sorted(range(1, self.n2), key=lambda step: abs(2 * step - self.n2))
        self.offsets1 = [
            (a, b, c) for a in ((1, 0) if self.fold else (0,)) for b in (1, 0) for c in (0, 1) if a + b + c
        ]


def kernel(
    plan, dims, factor,
    x_hbm, g_hbm, ws_hbm, wt_hbm,
    lo_hbm, gi_hbm, res_hbm,
    ws_ref, wt_ref, x_ext, xs, g_ext, hid, gp, gps, wf, wb, wtb, pre_s, gh_s, acc, part, slot1, slot2, fin, lo, gi,
    loc, xh_s, xh_r, gh_sem, gh_r, hd_s, hd_r, gp_s, gp_r, s1_s, s1_r, s2_s, s2_r, s3_s, s3_r,
):
    n_dp, n_tm, n_h = plan.n_dp, plan.n_tm, plan.n_h
    frames, rows, cols, ch = dims
    pix = rows * cols
    me_dp, me_tm, me_h = lax.axis_index("dp"), lax.axis_index("tm"), lax.axis_index("height")

    def remote(src, dst, send, recv, device):
        return pltpu.make_async_remote_copy(
            src_ref=src, dst_ref=dst, send_sem=send, recv_sem=recv, device_id=device, device_id_type=MESH,
        )

    def whole(ref, send, recv):
        return remote(ref, ref, send, recv, {"tm": me_tm})

    x_in = pltpu.make_async_copy(x_hbm.at[0], x_ext.at[:, pl.ds(1, rows)], loc.at[0])
    g_in = pltpu.make_async_copy(g_hbm.at[0], g_ext.at[pl.ds(0, frames)], loc.at[1])
    ws_in = pltpu.make_async_copy(ws_hbm, ws_ref, loc.at[2])
    wt_in = pltpu.make_async_copy(wt_hbm, wt_ref, loc.at[3])

    me_y, me_core = lax.div(me_tm, 2), lax.rem(me_tm, 2)

    def peer1(offset):
        a, b, c = offset
        dp = lax.rem(me_dp + a, 2) if plan.fold else me_dp
        tm = 2 * lax.rem(me_y + b, 2) + lax.rem(me_core + c, 2)
        return {"dp": dp, "tm": tm}, (dp * n_tm + tm if plan.fold else tm)

    me1 = me_dp * n_tm + me_tm if plan.fold else me_tm
    me2 = me_h if plan.fold else me_dp * n_h + me_h

    def peer2(step):
        index = lax.rem(me2 + step, plan.n2)
        if plan.fold:
            return {"height": index}, index
        return {"dp": lax.div(index, n_h), "height": lax.rem(index, n_h)}, index

    barrier = pltpu.get_barrier_semaphore()
    for step in range(1, plan.n2):
        pl.semaphore_signal(barrier, inc=1, device_id=peer2(step)[0], device_id_type=MESH)
    for offset in plan.offsets1:
        pl.semaphore_signal(barrier, inc=1, device_id=peer1(offset)[0], device_id_type=MESH)

    x_in.start()
    ws_in.start()
    wt_in.start()
    g_in.start()

    has_up, has_down = me_h > 0, me_h < n_h - 1
    has_prev, has_next = me_tm > 0, me_tm < n_tm - 1
    up, down = lax.rem(me_h + n_h - 1, n_h), lax.rem(me_h + 1, n_h)
    prev, nxt = lax.rem(me_tm + n_tm - 1, n_tm), lax.rem(me_tm + 1, n_tm)

    def x_copy(f, side):
        if side == 0:
            return remote(
                x_hbm.at[0, f, rows - 1], x_ext.at[f, 0], xh_s.at[0], xh_r.at[f, 0], {"height": down}
            )
        return remote(x_hbm.at[0, f, 0], x_ext.at[f, rows + 1], xh_s.at[1], xh_r.at[f, 1], {"height": up})

    def g_copy(f):
        return remote(g_hbm.at[0, f], g_ext.at[frames + f], gh_sem, gh_r.at[f], {"tm": prev})

    def h_copy(f):
        return remote(hid.at[f + 2], hid.at[f + 2 - frames], hd_s, hd_r, {"tm": nxt})

    def p_copy(f, side):
        if side == 0:
            return remote(gp.at[f, rows], gp.at[f, 0], gp_s.at[0], gp_r.at[f, 0], {"height": down})
        return remote(gp.at[f, 1], gp.at[f, rows + 1], gp_s.at[1], gp_r.at[f, 1], {"height": up})

    @pl.when(me_h == 0)
    def _():
        x_ext[:, 0] = jnp.zeros((frames, cols, ch), BF16)
        gp[:, 0] = jnp.zeros((frames, cols, ch), BF16)

    @pl.when(me_h == n_h - 1)
    def _():
        x_ext[:, rows + 1] = jnp.zeros((frames, cols, ch), BF16)
        gp[:, rows + 1] = jnp.zeros((frames, cols, ch), BF16)

    @pl.when(me_tm == 0)
    def _():
        hid[pl.ds(0, 2)] = jnp.zeros((2, rows, cols, ch), BF16)

    @pl.when(me_tm == n_tm - 1)
    def _():
        g_ext[pl.ds(frames, 2)] = jnp.zeros((2, rows, cols, ch), BF16)

    place = lax.broadcasted_iota(jnp.int32, (cols, ch), 0)

    def stack(source, target, f, r):
        value = source[f, r]
        wide = value.astype(F32)
        left = jnp.where(place == 0, 0.0, pltpu.roll(wide, 1, 0))
        right = jnp.where(place == cols - 1, 0.0, pltpu.roll(wide, cols - 1, 0))
        target[f, r, :, pl.ds(0, ch)] = left.astype(BF16)
        target[f, r, :, pl.ds(ch, ch)] = value
        target[f, r, :, pl.ds(2 * ch, ch)] = right.astype(BF16)

    def spread(source, weights, f, sources):
        sums = {}
        for s in sources:
            first, last = max(1, s - 1), min(rows, s + 1)
            at = first - s + 1
            wide = dot(source[f, s], weights[:, at * ch : (at + last - first + 1) * ch])
            for r in range(first, last + 1):
                term = wide[:, (r - first) * ch : (r - first + 1) * ch]
                sums[r] = sums[r] + term if r in sums else term
        return sums

    def beside(parts):
        return jnp.concatenate([p.reshape(pix, ch) for p in parts], axis=1)

    x_in.wait()

    @pl.loop(0, frames)
    def _(f):
        for r in range(1, rows + 1):
            stack(x_ext, xs, f, r)

    pl.semaphore_wait(barrier, plan.n2 - 1 + len(plan.offsets1))
    for f in range(2):
        pl.when(has_prev)(g_copy(f).start)
    for f in range(frames):
        pl.when(has_down)(x_copy(f, 0).start)
        pl.when(has_up)(x_copy(f, 1).start)

    ws_in.wait()
    wt_in.wait()
    for i in range(3):
        wf[:, pl.ds((2 - i) * ch, ch)] = ws_ref[i].reshape(3 * ch, ch)
        for j in range(3):
            wb[pl.ds((2 - j) * ch, ch), pl.ds(i * ch, ch)] = ws_ref[i, j].T
        wtb[pl.ds(i * ch, ch)] = wt_ref[i].T

    def row(f, r, pre):
        sigma = jax.nn.sigmoid(pre)
        hid[f + 2, r - 1] = (pre * sigma).astype(BF16)
        pre_s[f, r - 1] = sigma * (1.0 + pre * (1.0 - sigma))

    @pl.loop(0, frames)
    def _(f):
        for r, pre in spread(xs, wf, f, range(1, rows + 1)).items():
            if 1 < r < rows:
                row(f, r, pre)
            else:
                pre_s[f, r - 1] = pre

    g_in.wait()
    for f in range(frames):
        near = min(3, frames - f)
        value = dot(beside([g_ext[f + k] for k in range(near)]), wtb[pl.ds(0, near * ch)])
        gh_s[f] = value.reshape(rows, cols, ch)

    acc[...] = jnp.zeros(acc.shape, F32)

    def activate(f):
        pl.when(has_up)(x_copy(f, 0).wait_recv)
        pl.when(has_down)(x_copy(f, 1).wait_recv)
        for r in (0, rows + 1):
            stack(x_ext, xs, f, r)
        for r, value in spread(xs, wf, f, (0, rows + 1)).items():
            row(f, r, pre_s[f, r - 1] + value)

    def back(f):
        near = min(3, frames - f)
        far = None
        if near < 3:
            far = dot(beside([g_ext[f + k] for k in range(near, 3)]), wtb[pl.ds(near * ch, (3 - near) * ch)])
            far = far.reshape(rows, cols, ch)
        for r in range(1, rows + 1):
            grad_hidden = gh_s[f, r - 1]
            if far is not None:
                grad_hidden = grad_hidden + far[r - 1]
            gp[f, r] = (grad_hidden * pre_s[f, r - 1]).astype(BF16)
            stack(gp, gps, f, r)

    def p_start(f):
        pl.when(has_down)(p_copy(f, 0).start)
        pl.when(has_up)(p_copy(f, 1).start)

    def temporal_grad(f):
        term = tdot(hid[f + 2].reshape(pix, ch), beside([g_ext[f + k] for k in range(3)]))
        for k in range(3):
            acc[pl.ds((9 + k) * ch, ch)] += term[:, k * ch : (k + 1) * ch]

    def spatial_grad(f):
        term = tdot(
            beside([x_ext[f, pl.ds(i, rows)] for i in range(3)]),
            gps[f, pl.ds(1, rows)].reshape(pix, 3 * ch),
        )
        for j in range(3):
            acc[pl.ds(3 * j * ch, 3 * ch)] += term[:, (2 - j) * ch : (3 - j) * ch]

    n_chunks = len(plan.chunks)
    temporal = n_chunks - 1

    def s1_copy(c, k):
        base, size = plan.chunks[c]
        piece = size // plan.n1
        device, index = peer1(plan.offsets1[k])
        return remote(
            part.at[pl.ds(pl.multiple_of(base + index * piece, 16), piece)],
            slot1.at[c, k], s1_s, s1_r.at[c], device,
        )

    def scatter(c):
        base, size = plan.chunks[c]
        part[pl.ds(base, size)] = acc[pl.ds(base, size)].astype(BF16)
        for k in range(len(plan.offsets1)):
            s1_copy(c, k).start()

    def s2_copy(c, step):
        device, _ = peer2(step)
        at = slot2.at[c, me2]
        return remote(at, at, s2_s, s2_r.at[c], device)

    def exchange(c):
        base, size = plan.chunks[c]
        piece = size // plan.n1
        total = acc[pl.ds(pl.multiple_of(base + me1 * piece, 16), piece)]
        whole(slot1.at[c], s1_s, s1_r.at[c]).wait_recv()
        for k in range(len(plan.offsets1)):
            total = total + slot1[c, k].astype(F32)
        slot2[c, me2] = total.astype(BF16)
        for step in plan.steps2:
            s2_copy(c, step).start()

    def s3_copy(c, k):
        base, size = plan.chunks[c]
        piece = size // plan.n1
        at = res_hbm.at[pl.ds(pl.multiple_of(base + me1 * piece, 16), piece)]
        return remote(fin.at[c], at, s3_s, s3_r.at[c], peer1(plan.offsets1[k])[0])

    def s3_own(c):
        base, size = plan.chunks[c]
        piece = size // plan.n1
        at = res_hbm.at[pl.ds(pl.multiple_of(base + me1 * piece, 16), piece)]
        return pltpu.make_async_copy(fin.at[c], at, loc.at[6])

    def gather(c):
        whole(slot2.at[c, pl.ds(0, plan.n2 - 1)], s2_s, s2_r.at[c]).wait_recv()
        total = slot2[c, 0].astype(F32)
        for source in range(1, plan.n2):
            total = total + slot2[c, source].astype(F32)
        fin[c] = (total * factor).astype(BF16)
        for k in range(len(plan.offsets1)):
            s3_copy(c, k).start()
        s3_own(c).start()

    lo_out = pltpu.make_async_copy(lo, lo_hbm.at[0], loc.at[4])

    def gi_copy(f):
        return pltpu.make_async_copy(gi.at[f], gi_hbm.at[0, f], loc.at[5])

    def grad_in(f):
        pl.when(has_up)(p_copy(f, 0).wait_recv)
        pl.when(has_down)(p_copy(f, 1).wait_recv)
        for r in (0, rows + 1):
            stack(gp, gps, f, r)
        for r, value in spread(gps, wb, f, range(rows + 2)).items():
            gi[f, r - 1] = value.astype(BF16)
        gi_copy(f).start()

    def layer(f):
        mixed = dot(beside([hid[f + 2], hid[f + 1], hid[f]]), wt_ref[...].reshape(3 * ch, ch))
        lo[f] = mixed.astype(BF16).reshape(rows, cols, ch)

    for f in range(frames):
        activate(f)
        if f == frames - 2:
            pl.when(has_next)(h_copy(f).start)
        if f + 2 >= frames:
            pl.when(has_next)(g_copy(f + 2 - frames).wait_recv)
        back(f)
        if f < frames - 1:
            p_start(f)
        temporal_grad(f)
        if f == frames - 1:
            scatter(temporal)
        spatial_grad(f)

    for c in range(temporal):
        scatter(c)
    for f in range(frames - 1):
        grad_in(f)
    for c in (temporal, *range(temporal)):
        exchange(c)
    p_start(frames - 1)
    pl.when(has_next)(h_copy(frames - 1).start)
    layer(frames - 1)
    for c in (temporal, *range(temporal)):
        gather(c)
    grad_in(frames - 1)

    pl.when(has_prev)(whole(hid.at[pl.ds(0, 2)], hd_s, hd_r).wait_recv)

    for f in range(frames - 1):
        layer(f)
    lo_out.start()

    pl.when(has_down)(whole(x_ext.at[:, 0], xh_s.at[0], xh_r.at[0, 0]).wait_send)
    pl.when(has_up)(whole(x_ext.at[:, 0], xh_s.at[1], xh_r.at[0, 0]).wait_send)
    pl.when(has_down)(whole(gp.at[:, 0], gp_s.at[0], gp_r.at[0, 0]).wait_send)
    pl.when(has_up)(whole(gp.at[:, 0], gp_s.at[1], gp_r.at[0, 0]).wait_send)
    pl.when(has_prev)(whole(g_ext.at[pl.ds(0, 2)], gh_sem, gh_r.at[0]).wait_send)
    pl.when(has_next)(whole(hid.at[pl.ds(0, 2)], hd_s, hd_r).wait_send)
    whole(slot1, s1_s, s1_r.at[0]).wait_send()
    whole(slot2.at[:, pl.ds(0, plan.n2 - 1)], s2_s, s2_r.at[0]).wait_send()
    pltpu.make_async_copy(gi, gi_hbm.at[0], loc.at[5]).wait()
    lo_out.wait()
    pltpu.make_async_copy(fin, fin, loc.at[6]).wait()
    for c in (temporal, *range(temporal)):
        whole(slot1.at[c], s3_s, s3_r.at[c]).wait_recv()
    whole(slot1, s3_s, s3_r.at[0]).wait_send()


def finish(frames, ch, lo, gi, res, lo_hbm, gi_hbm, gs_hbm, gt_hbm, gs, gt, sem):
    copies = []
    for source, target in ((lo, lo_hbm), (gi, gi_hbm)):
        for f in range(frames):
            copies.append(pltpu.make_async_copy(source.at[0, f], target.at[0, f], sem.at[len(copies)]))
    for copy in copies:
        copy.start()
    for i in range(3):
        for j in range(3):
            gs[i, j] = res[pl.ds((3 * j + i) * ch, ch)].astype(F32)
        copies.append(pltpu.make_async_copy(gs.at[i], gs_hbm.at[i], sem.at[len(copies)]))
        copies[-1].start()
    gt[...] = res[pl.ds(9 * ch, 3 * ch)].astype(F32).reshape(3, ch, ch)
    copies.append(pltpu.make_async_copy(gt, gt_hbm, sem.at[len(copies)]))
    copies[-1].start()
    for copy in copies:
        copy.wait()


def per_device(sizes, frames_in, grad_out, w_spatial, w_temporal):
    clips, frames, rows, cols, ch = frames_in.shape
    n_dp, n_tm, n_h = sizes
    assert clips == 1 and n_tm == 4 and frames > 2 and rows > 1
    plan = Plan(sizes, ch)
    n_chunks, peers1 = len(plan.chunks), len(plan.offsets1)
    factor = 1.0 / math.sqrt(clips * frames * rows * cols * n_dp * n_tm * n_h)
    operands = [
        pltpu.with_memory_space_constraint(a, pltpu.HBM)
        for a in (frames_in, grad_out, w_spatial, w_temporal)
    ]
    any_spec = pl.BlockSpec(memory_space=pl.ANY)
    vmem_spec = pl.BlockSpec(memory_space=pltpu.VMEM)
    hbm_spec = pl.BlockSpec(memory_space=pltpu.HBM)
    dma = pltpu.SemaphoreType.DMA
    block = jax.ShapeDtypeStruct(frames_in.shape, BF16)
    layer_out, grad_in, sums = pl.pallas_call(
        functools.partial(kernel, plan, (frames, rows, cols, ch), factor),
        out_shape=(block, block, jax.ShapeDtypeStruct((12 * ch, ch), BF16)),
        in_specs=[any_spec] * 4,
        out_specs=(any_spec, any_spec, any_spec),
        scratch_shapes=[
            pltpu.VMEM((3, 3, ch, ch), BF16),
            pltpu.VMEM((3, ch, ch), BF16),
            pltpu.VMEM((frames, rows + 2, cols, ch), BF16),
            pltpu.VMEM((frames, rows + 2, cols, 3 * ch), BF16),
            pltpu.VMEM((frames + 2, rows, cols, ch), BF16),
            pltpu.VMEM((frames + 2, rows, cols, ch), BF16),
            pltpu.VMEM((frames, rows + 2, cols, ch), BF16),
            pltpu.VMEM((frames, rows + 2, cols, 3 * ch), BF16),
            pltpu.VMEM((3 * ch, 3 * ch), BF16),
            pltpu.VMEM((3 * ch, 3 * ch), BF16),
            pltpu.VMEM((3 * ch, ch), BF16),
            pltpu.VMEM((frames, rows, cols, ch), F32),
            pltpu.VMEM((frames, rows, cols, ch), F32),
            pltpu.VMEM((12 * ch, ch), F32),
            pltpu.VMEM((12 * ch, ch), BF16),
            pltpu.VMEM((n_chunks, peers1, plan.piece, ch), BF16),
            pltpu.VMEM((n_chunks, plan.n2, plan.piece, ch), BF16),
            pltpu.VMEM((n_chunks, plan.piece, ch), BF16),
            pltpu.VMEM((frames, rows, cols, ch), BF16),
            pltpu.VMEM((frames, rows, cols, ch), BF16),
            dma((7,)),
            dma((2,)), dma((frames, 2)), dma, dma((2,)), dma, dma, dma((2,)), dma((frames, 2)),
            dma, dma((n_chunks,)), dma, dma((n_chunks,)), dma, dma((n_chunks,)),
        ],
        compiler_params=pltpu.CompilerParams(
            collective_id=0, has_side_effects=True, vmem_limit_bytes=48 << 20
        ),
    )(*operands)
    return pl.pallas_call(
        functools.partial(finish, frames, ch),
        out_shape=(
            block, block,
            jax.ShapeDtypeStruct((3, 3, ch, ch), F32), jax.ShapeDtypeStruct((3, ch, ch), F32),
        ),
        in_specs=[vmem_spec] * 3,
        out_specs=(hbm_spec,) * 4,
        scratch_shapes=[
            pltpu.VMEM((3, 3, ch, ch), F32), pltpu.VMEM((3, ch, ch), F32), dma((2 * frames + 4,)),
        ],
        compiler_params=pltpu.CompilerParams(vmem_limit_bytes=16 << 20),
    )(layer_out, grad_in, sums)


def solution(mesh):
    sizes = (mesh.shape["dp"], mesh.shape["tm"], mesh.shape["height"])
    spec = P("dp", "tm", "height", None, None)
    return jax.shard_map(
        functools.partial(per_device, sizes), mesh=mesh,
        in_specs=(spec, spec, P(), P()), out_specs=(spec, spec, P(), P()), check_vma=False,
    )
```

```python
import functools
import math

import jax
import jax.numpy as jnp
from jax import lax
from jax.experimental import pallas as pl
from jax.experimental.pallas import tpu as pltpu
from jax.sharding import PartitionSpec as P

F32, BF16 = jnp.float32, jnp.bfloat16
MESH = pl.DeviceIdType.MESH
SPATIAL_CHUNKS = 3


def tdot(lhs, rhs):
    return lax.dot_general(lhs, rhs, (((0,), (0,)), ((), ())), preferred_element_type=F32)


def dot(lhs, rhs):
    return jnp.dot(lhs, rhs, preferred_element_type=F32)


class Plan:
    def __init__(self, sizes, ch):
        self.n_dp, self.n_tm, self.n_h = sizes
        self.fold = self.n_dp == 2
        self.n1 = self.n_tm * (self.n_dp if self.fold else 1)
        self.n2 = self.n_h * (1 if self.fold else self.n_dp)
        size = 9 * ch // SPATIAL_CHUNKS
        self.chunks = [(size * k, size) for k in range(SPATIAL_CHUNKS)] + [(9 * ch, 3 * ch)]
        assert all(rows == size for _, rows in self.chunks) and size % (16 * self.n1) == 0
        self.piece = size // self.n1
        self.steps2 = sorted(range(1, self.n2), key=lambda step: abs(2 * step - self.n2))
        self.offsets1 = [
            (a, b, c) for a in ((1, 0) if self.fold else (0,)) for b in (1, 0) for c in (0, 1) if a + b + c
        ]


def kernel(
    plan, dims, factor,
    x_hbm, g_hbm, ws_hbm, wt_hbm,
    lo_hbm, gi_hbm, res_hbm,
    ws_ref, wt_ref, x_ext, xs, g_ext, hid, gp, gps, wf, wb, wtb, pre_s, gh_s, acc, part, slot1, slot2, fin, lo, gi,
    loc, xh_s, xh_r, gh_sem, gh_r, hd_s, hd_r, gp_s, gp_r, s1_s, s1_r, s2_s, s2_r, s3_s, s3_r,
):
    n_dp, n_tm, n_h = plan.n_dp, plan.n_tm, plan.n_h
    frames, rows, cols, ch = dims
    pix = rows * cols
    me_dp, me_tm, me_h = lax.axis_index("dp"), lax.axis_index("tm"), lax.axis_index("height")

    def remote(src, dst, send, recv, device):
        return pltpu.make_async_remote_copy(
            src_ref=src, dst_ref=dst, send_sem=send, recv_sem=recv, device_id=device, device_id_type=MESH,
        )

    def whole(ref, send, recv):
        return remote(ref, ref, send, recv, {"tm": me_tm})

    x_in = pltpu.make_async_copy(x_hbm.at[0], x_ext.at[:, pl.ds(1, rows)], loc.at[0])
    g_in = pltpu.make_async_copy(g_hbm.at[0], g_ext.at[pl.ds(0, frames)], loc.at[1])
    ws_in = pltpu.make_async_copy(ws_hbm, ws_ref, loc.at[2])
    wt_in = pltpu.make_async_copy(wt_hbm, wt_ref, loc.at[3])
    x_in.start()
    ws_in.start()
    wt_in.start()
    g_in.start()

    me_y, me_core = lax.div(me_tm, 2), lax.rem(me_tm, 2)

    def peer1(offset):
        a, b, c = offset
        dp = lax.rem(me_dp + a, 2) if plan.fold else me_dp
        tm = 2 * lax.rem(me_y + b, 2) + lax.rem(me_core + c, 2)
        return {"dp": dp, "tm": tm}, (dp * n_tm + tm if plan.fold else tm)

    me1 = me_dp * n_tm + me_tm if plan.fold else me_tm
    me2 = me_h if plan.fold else me_dp * n_h + me_h

    def peer2(step):
        index = lax.rem(me2 + step, plan.n2)
        if plan.fold:
            return {"height": index}, index
        return {"dp": lax.div(index, n_h), "height": lax.rem(index, n_h)}, index

    barrier = pltpu.get_barrier_semaphore()
    for step in range(1, plan.n2):
        pl.semaphore_signal(barrier, inc=1, device_id=peer2(step)[0], device_id_type=MESH)
    for offset in plan.offsets1:
        pl.semaphore_signal(barrier, inc=1, device_id=peer1(offset)[0], device_id_type=MESH)

    has_up, has_down = me_h > 0, me_h < n_h - 1
    has_prev, has_next = me_tm > 0, me_tm < n_tm - 1
    up, down = lax.rem(me_h + n_h - 1, n_h), lax.rem(me_h + 1, n_h)
    prev, nxt = lax.rem(me_tm + n_tm - 1, n_tm), lax.rem(me_tm + 1, n_tm)

    def x_copy(f, side):
        if side == 0:
            return remote(
                x_hbm.at[0, f, rows - 1], x_ext.at[f, 0], xh_s.at[0], xh_r.at[f, 0], {"height": down}
            )
        return remote(x_hbm.at[0, f, 0], x_ext.at[f, rows + 1], xh_s.at[1], xh_r.at[f, 1], {"height": up})

    def g_copy(f):
        return remote(g_hbm.at[0, f], g_ext.at[frames + f], gh_sem, gh_r.at[f], {"tm": prev})

    def h_copy(f):
        return remote(hid.at[f + 2], hid.at[f + 2 - frames], hd_s, hd_r, {"tm": nxt})

    def p_copy(f, side):
        if side == 0:
            return remote(gp.at[f, rows], gp.at[f, 0], gp_s.at[0], gp_r.at[f, 0], {"height": down})
        return remote(gp.at[f, 1], gp.at[f, rows + 1], gp_s.at[1], gp_r.at[f, 1], {"height": up})

    @pl.when(me_h == 0)
    def _():
        x_ext[:, 0] = jnp.zeros((frames, cols, ch), BF16)
        gp[:, 0] = jnp.zeros((frames, cols, ch), BF16)

    @pl.when(me_h == n_h - 1)
    def _():
        x_ext[:, rows + 1] = jnp.zeros((frames, cols, ch), BF16)
        gp[:, rows + 1] = jnp.zeros((frames, cols, ch), BF16)

    @pl.when(me_tm == 0)
    def _():
        hid[pl.ds(0, 2)] = jnp.zeros((2, rows, cols, ch), BF16)

    @pl.when(me_tm == n_tm - 1)
    def _():
        g_ext[pl.ds(frames, 2)] = jnp.zeros((2, rows, cols, ch), BF16)

    place = lax.broadcasted_iota(jnp.int32, (cols, ch), 0)

    def stack(source, target, f, r):
        value = source[f, r]
        wide = value.astype(F32)
        left = jnp.where(place == 0, 0.0, pltpu.roll(wide, 1, 0))
        right = jnp.where(place == cols - 1, 0.0, pltpu.roll(wide, cols - 1, 0))
        target[f, r, :, pl.ds(0, ch)] = left.astype(BF16)
        target[f, r, :, pl.ds(ch, ch)] = value
        target[f, r, :, pl.ds(2 * ch, ch)] = right.astype(BF16)

    def spread(source, weights, f, sources):
        sums = {}
        for s in sources:
            first, last = max(1, s - 1), min(rows, s + 1)
            at = first - s + 1
            wide = dot(source[f, s], weights[:, at * ch : (at + last - first + 1) * ch])
            for r in range(first, last + 1):
                term = wide[:, (r - first) * ch : (r - first + 1) * ch]
                sums[r] = sums[r] + term if r in sums else term
        return sums

    def beside(parts):
        return jnp.concatenate([p.reshape(pix, ch) for p in parts], axis=1)

    x_in.wait()

    @pl.loop(0, frames)
    def _(f):
        for r in range(1, rows + 1):
            stack(x_ext, xs, f, r)

    pl.semaphore_wait(barrier, plan.n2 - 1 + len(plan.offsets1))
    for f in range(frames):
        pl.when(has_down)(x_copy(f, 0).start)
        pl.when(has_up)(x_copy(f, 1).start)
    for f in range(2):
        pl.when(has_prev)(g_copy(f).start)

    ws_in.wait()
    wt_in.wait()
    for i in range(3):
        wf[:, pl.ds((2 - i) * ch, ch)] = ws_ref[i].reshape(3 * ch, ch)
        for j in range(3):
            wb[pl.ds((2 - j) * ch, ch), pl.ds(i * ch, ch)] = ws_ref[i, j].T
        wtb[pl.ds(i * ch, ch)] = wt_ref[i].T

    @pl.loop(0, frames)
    def _(f):
        for r, value in spread(xs, wf, f, range(1, rows + 1)).items():
            pre_s[f, r - 1] = value

    g_in.wait()
    for f in range(frames):
        near = min(3, frames - f)
        value = dot(beside([g_ext[f + k] for k in range(near)]), wtb[pl.ds(0, near * ch)])
        gh_s[f] = value.reshape(rows, cols, ch)

    acc[...] = jnp.zeros(acc.shape, F32)

    def activate(f):
        pl.when(has_up)(x_copy(f, 0).wait_recv)
        pl.when(has_down)(x_copy(f, 1).wait_recv)
        for r in (0, rows + 1):
            stack(x_ext, xs, f, r)
        edge = spread(xs, wf, f, (0, rows + 1))
        for r in range(1, rows + 1):
            pre = pre_s[f, r - 1]
            if r in edge:
                pre = pre + edge[r]
            sigma = 0.5 + 0.5 * jnp.tanh(0.5 * pre)
            hid[f + 2, r - 1] = (pre * sigma).astype(BF16)
            pre_s[f, r - 1] = sigma * (1.0 + pre * (1.0 - sigma))

    def back(f):
        near = min(3, frames - f)
        far = None
        if near < 3:
            far = dot(beside([g_ext[f + k] for k in range(near, 3)]), wtb[pl.ds(near * ch, (3 - near) * ch)])
            far = far.reshape(rows, cols, ch)
        for r in range(1, rows + 1):
            grad_hidden = gh_s[f, r - 1]
            if far is not None:
                grad_hidden = grad_hidden + far[r - 1]
            gp[f, r] = (grad_hidden * pre_s[f, r - 1]).astype(BF16)
            stack(gp, gps, f, r)

    def p_start(f):
        pl.when(has_down)(p_copy(f, 0).start)
        pl.when(has_up)(p_copy(f, 1).start)

    def temporal_grad(f):
        term = tdot(hid[f + 2].reshape(pix, ch), beside([g_ext[f + k] for k in range(3)]))
        for k in range(3):
            acc[pl.ds((9 + k) * ch, ch)] += term[:, k * ch : (k + 1) * ch]

    def spatial_grad(f):
        term = tdot(
            beside([x_ext[f, pl.ds(i, rows)] for i in range(3)]),
            gps[f, pl.ds(1, rows)].reshape(pix, 3 * ch),
        )
        for j in range(3):
            acc[pl.ds(3 * j * ch, 3 * ch)] += term[:, (2 - j) * ch : (3 - j) * ch]

    n_chunks = len(plan.chunks)
    temporal = n_chunks - 1

    def s1_copy(c, k):
        base, size = plan.chunks[c]
        piece = size // plan.n1
        device, index = peer1(plan.offsets1[k])
        return remote(
            part.at[pl.ds(pl.multiple_of(base + index * piece, 16), piece)],
            slot1.at[c, k], s1_s, s1_r.at[c], device,
        )

    def scatter(c):
        base, size = plan.chunks[c]
        part[pl.ds(base, size)] = acc[pl.ds(base, size)].astype(BF16)
        for k in range(len(plan.offsets1)):
            s1_copy(c, k).start()

    def s2_copy(c, step):
        device, _ = peer2(step)
        at = slot2.at[c, me2]
        return remote(at, at, s2_s, s2_r.at[c], device)

    def exchange(c):
        base, size = plan.chunks[c]
        piece = size // plan.n1
        total = acc[pl.ds(pl.multiple_of(base + me1 * piece, 16), piece)]
        whole(slot1.at[c], s1_s, s1_r.at[c]).wait_recv()
        for k in range(len(plan.offsets1)):
            total = total + slot1[c, k].astype(F32)
        slot2[c, me2] = total.astype(BF16)
        for step in plan.steps2:
            s2_copy(c, step).start()

    def s3_copy(c, k):
        base, size = plan.chunks[c]
        piece = size // plan.n1
        at = res_hbm.at[pl.ds(pl.multiple_of(base + me1 * piece, 16), piece)]
        return remote(fin.at[c], at, s3_s, s3_r.at[c], peer1(plan.offsets1[k])[0])

    def s3_own(c):
        base, size = plan.chunks[c]
        piece = size // plan.n1
        at = res_hbm.at[pl.ds(pl.multiple_of(base + me1 * piece, 16), piece)]
        return pltpu.make_async_copy(fin.at[c], at, loc.at[6])

    def gather(c):
        whole(slot2.at[c, pl.ds(0, plan.n2 - 1)], s2_s, s2_r.at[c]).wait_recv()
        total = slot2[c, 0].astype(F32)
        for source in range(1, plan.n2):
            total = total + slot2[c, source].astype(F32)
        fin[c] = (total * factor).astype(BF16)
        for k in range(len(plan.offsets1)):
            s3_copy(c, k).start()
        s3_own(c).start()

    lo_out = pltpu.make_async_copy(lo, lo_hbm.at[0], loc.at[4])

    def gi_copy(f):
        return pltpu.make_async_copy(gi.at[f], gi_hbm.at[0, f], loc.at[5])

    def grad_in(f):
        pl.when(has_up)(p_copy(f, 0).wait_recv)
        pl.when(has_down)(p_copy(f, 1).wait_recv)
        for r in (0, rows + 1):
            stack(gp, gps, f, r)
        for r, value in spread(gps, wb, f, range(rows + 2)).items():
            gi[f, r - 1] = value.astype(BF16)
        gi_copy(f).start()

    def layer(f):
        mixed = dot(beside([hid[f + 2], hid[f + 1], hid[f]]), wt_ref[...].reshape(3 * ch, ch))
        lo[f] = mixed.astype(BF16).reshape(rows, cols, ch)

    for f in range(frames):
        activate(f)
        if f == frames - 2:
            pl.when(has_next)(h_copy(f).start)
        if f + 2 >= frames:
            pl.when(has_next)(g_copy(f + 2 - frames).wait_recv)
        back(f)
        if f < frames - 1:
            p_start(f)
        temporal_grad(f)
        if f == frames - 1:
            scatter(temporal)
        spatial_grad(f)

    for c in range(temporal):
        scatter(c)
    for f in range(frames - 1):
        grad_in(f)
    for c in (temporal, *range(temporal)):
        exchange(c)
    p_start(frames - 1)
    pl.when(has_next)(h_copy(frames - 1).start)
    layer(frames - 1)
    for c in (temporal, *range(temporal)):
        gather(c)
    grad_in(frames - 1)

    pl.when(has_prev)(whole(hid.at[pl.ds(0, 2)], hd_s, hd_r).wait_recv)

    for f in range(frames - 1):
        layer(f)
    lo_out.start()

    pl.when(has_down)(whole(x_ext.at[:, 0], xh_s.at[0], xh_r.at[0, 0]).wait_send)
    pl.when(has_up)(whole(x_ext.at[:, 0], xh_s.at[1], xh_r.at[0, 0]).wait_send)
    pl.when(has_down)(whole(gp.at[:, 0], gp_s.at[0], gp_r.at[0, 0]).wait_send)
    pl.when(has_up)(whole(gp.at[:, 0], gp_s.at[1], gp_r.at[0, 0]).wait_send)
    pl.when(has_prev)(whole(g_ext.at[pl.ds(0, 2)], gh_sem, gh_r.at[0]).wait_send)
    pl.when(has_next)(whole(hid.at[pl.ds(0, 2)], hd_s, hd_r).wait_send)
    whole(slot1, s1_s, s1_r.at[0]).wait_send()
    whole(slot2.at[:, pl.ds(0, plan.n2 - 1)], s2_s, s2_r.at[0]).wait_send()
    pltpu.make_async_copy(gi, gi_hbm.at[0], loc.at[5]).wait()
    lo_out.wait()
    pltpu.make_async_copy(fin, fin, loc.at[6]).wait()
    for c in (temporal, *range(temporal)):
        whole(slot1.at[c], s3_s, s3_r.at[c]).wait_recv()
    whole(slot1, s3_s, s3_r.at[0]).wait_send()


def finish(frames, ch, lo, gi, res, lo_hbm, gi_hbm, gs_hbm, gt_hbm, gs, gt, sem):
    copies = []
    for source, target in ((lo, lo_hbm), (gi, gi_hbm)):
        for f in range(frames):
            copies.append(pltpu.make_async_copy(source.at[0, f], target.at[0, f], sem.at[len(copies)]))
    for copy in copies:
        copy.start()
    for i in range(3):
        for j in range(3):
            gs[i, j] = res[pl.ds((3 * j + i) * ch, ch)].astype(F32)
        copies.append(pltpu.make_async_copy(gs.at[i], gs_hbm.at[i], sem.at[len(copies)]))
        copies[-1].start()
    gt[...] = res[pl.ds(9 * ch, 3 * ch)].astype(F32).reshape(3, ch, ch)
    copies.append(pltpu.make_async_copy(gt, gt_hbm, sem.at[len(copies)]))
    copies[-1].start()
    for copy in copies:
        copy.wait()


def per_device(sizes, frames_in, grad_out, w_spatial, w_temporal):
    clips, frames, rows, cols, ch = frames_in.shape
    n_dp, n_tm, n_h = sizes
    assert clips == 1 and n_tm == 4 and frames > 2 and rows > 1
    plan = Plan(sizes, ch)
    n_chunks, peers1 = len(plan.chunks), len(plan.offsets1)
    factor = 1.0 / math.sqrt(clips * frames * rows * cols * n_dp * n_tm * n_h)
    operands = [
        pltpu.with_memory_space_constraint(a, pltpu.HBM)
        for a in (frames_in, grad_out, w_spatial, w_temporal)
    ]
    any_spec = pl.BlockSpec(memory_space=pl.ANY)
    vmem_spec = pl.BlockSpec(memory_space=pltpu.VMEM)
    hbm_spec = pl.BlockSpec(memory_space=pltpu.HBM)
    dma = pltpu.SemaphoreType.DMA
    block = jax.ShapeDtypeStruct(frames_in.shape, BF16)
    layer_out, grad_in, sums = pl.pallas_call(
        functools.partial(kernel, plan, (frames, rows, cols, ch), factor),
        out_shape=(block, block, jax.ShapeDtypeStruct((12 * ch, ch), BF16)),
        in_specs=[any_spec] * 4,
        out_specs=(any_spec, any_spec, any_spec),
        scratch_shapes=[
            pltpu.VMEM((3, 3, ch, ch), BF16),
            pltpu.VMEM((3, ch, ch), BF16),
            pltpu.VMEM((frames, rows + 2, cols, ch), BF16),
            pltpu.VMEM((frames, rows + 2, cols, 3 * ch), BF16),
            pltpu.VMEM((frames + 2, rows, cols, ch), BF16),
            pltpu.VMEM((frames + 2, rows, cols, ch), BF16),
            pltpu.VMEM((frames, rows + 2, cols, ch), BF16),
            pltpu.VMEM((frames, rows + 2, cols, 3 * ch), BF16),
            pltpu.VMEM((3 * ch, 3 * ch), BF16),
            pltpu.VMEM((3 * ch, 3 * ch), BF16),
            pltpu.VMEM((3 * ch, ch), BF16),
            pltpu.VMEM((frames, rows, cols, ch), F32),
            pltpu.VMEM((frames, rows, cols, ch), F32),
            pltpu.VMEM((12 * ch, ch), F32),
            pltpu.VMEM((12 * ch, ch), BF16),
            pltpu.VMEM((n_chunks, peers1, plan.piece, ch), BF16),
            pltpu.VMEM((n_chunks, plan.n2, plan.piece, ch), BF16),
            pltpu.VMEM((n_chunks, plan.piece, ch), BF16),
            pltpu.VMEM((frames, rows, cols, ch), BF16),
            pltpu.VMEM((frames, rows, cols, ch), BF16),
            dma((7,)),
            dma((2,)), dma((frames, 2)), dma, dma((2,)), dma, dma, dma((2,)), dma((frames, 2)),
            dma, dma((n_chunks,)), dma, dma((n_chunks,)), dma, dma((n_chunks,)),
        ],
        compiler_params=pltpu.CompilerParams(
            collective_id=0, has_side_effects=True, vmem_limit_bytes=48 << 20
        ),
    )(*operands)
    return pl.pallas_call(
        functools.partial(finish, frames, ch),
        out_shape=(
            block, block,
            jax.ShapeDtypeStruct((3, 3, ch, ch), F32), jax.ShapeDtypeStruct((3, ch, ch), F32),
        ),
        in_specs=[vmem_spec] * 3,
        out_specs=(hbm_spec,) * 4,
        scratch_shapes=[
            pltpu.VMEM((3, 3, ch, ch), F32), pltpu.VMEM((3, ch, ch), F32), dma((2 * frames + 4,)),
        ],
        compiler_params=pltpu.CompilerParams(vmem_limit_bytes=16 << 20),
    )(layer_out, grad_in, sums)


def solution(mesh):
    sizes = (mesh.shape["dp"], mesh.shape["tm"], mesh.shape["height"])
    spec = P("dp", "tm", "height", None, None)
    return jax.shard_map(
        functools.partial(per_device, sizes), mesh=mesh,
        in_specs=(spec, spec, P(), P()), out_specs=(spec, spec, P(), P()), check_vma=False,
    )
```
